32 devices in a mesh: lat: 4 (over y, x), lon: 8 (over z, core).
Axes of the slice: x: 2, y: 2, z: 4, core: 2. Of those that a mesh axis runs over, the one named last changes fastest.
Arguments:
- features: bfloat16 [4, 96, 96, 512], P(None, 'lat', 'lon'), may hold values from -6 to 6
- packed_first: bfloat16 [512, 1536], replicated, may hold values from -0.25 to 0.25
- scale_first: float32 [8], replicated, may hold values from 2 to 16
- output_first: bfloat16 [512, 512], replicated, may hold values from -0.25 to 0.25
- gain_first: float32 [512], replicated, may hold values from 0.5 to 1.5
- offset_first: float32 [512], replicated, may hold values from -1.5 to 1.5
- merge_weight: bfloat16 [2048, 1024], replicated, may hold values from -0.125 to 0.125
- merge_gain: float32 [1024], replicated, may hold values from 0.5 to 1.5
- merge_offset: float32 [1024], replicated, may hold values from -1.5 to 1.5
- packed_second: bfloat16 [1024, 1536], replicated, may hold values from -0.1875 to 0.1875
- scale_second: float32 [8], replicated, may hold values from 2 to 16
- output_second: bfloat16 [512, 1024], replicated, may hold values from -0.25 to 0.25
- gain_second: float32 [1024], replicated, may hold values from 0.5 to 1.5
- offset_second: float32 [1024], replicated, may hold values from -1.5 to 1.5
Outputs:
- coarse_out: bfloat16 [48, 8, 2, 12, 1024], P('lat', 'lon')
The draws below stay inside these ranges and needn't reach their ends.
All inputs are finite; a program needn't handle non-finite values.
Results may differ from the reference program's by a relative error of at most 0.019.
Values may be sent and summed in bfloat16 or wider, within the bound.
No kernel may reach another device: no remote copies, remote signals or barrier semaphores. Data moves between devices by JAX's collectives and lax.ppermute only.
A program may use at most 128 MiB of HBM per device.

```python
import math
import jax
import jax.numpy as jnp
from jax import lax

LEVELS = 4
WLEV = 2
WLAT = 6
WLON = 12
HD = 64
HEADS1 = 8
HEADS2 = 8
D1 = 512
D2 = 1024
NLAT = 96
NLON = 96


def shard_levels(key, dims, shards, low, top_value):
    level, own = 1.0, jax.random.fold_in(key, 6)
    for axis_at, shards_of in shards:
        draws = jnp.exp(jax.random.uniform(jax.random.fold_in(own, axis_at), (shards_of,), jnp.float32, low / len(shards), top_value / len(shards)))
        level = level * jnp.repeat(draws, dims[axis_at] // shards_of).reshape([-1 if axis == axis_at else 1 for axis in range(len(dims))])
    return level


def gaussian(rng, dims, scale, bound, shards=(), dtype=jnp.bfloat16):
    values = jax.random.normal(rng, dims, jnp.float32) * scale
    if len(shards) > 0:
        values = shard_levels(rng, dims, shards, -0.22, 0.18) * values
    return jnp.clip(values, min=-bound, max=bound).astype(dtype)


def setup_inputs(seed: int = 0) -> dict:
    streams_of = jax.random.split(jax.random.key(seed), 15)
    return {
        "features": gaussian(streams_of[0], (LEVELS, NLAT, NLON, D1), 1.0, 6.0, ((1, 4), (2, 8))),
        "packed_first": gaussian(streams_of[1], (D1, 3 * HEADS1 * HD), D1 ** -0.5, 0.25),
        "scale_first": jnp.clip(jnp.exp(jax.random.uniform(streams_of[2], (HEADS1,), jnp.float32, math.log(2.0), math.log(16.0))), 2.0, 16.0),
        "output_first": gaussian(streams_of[3], (HEADS1 * HD, D1), (HEADS1 * HD) ** -0.5, 0.25),
        "gain_first": jnp.clip(1.0 + 0.1 * jax.random.normal(streams_of[4], (D1,), jnp.float32), 0.5, 1.5),
        "offset_first": gaussian(streams_of[5], (D1,), 0.3, 1.5, (), jnp.float32),
        "merge_weight": gaussian(streams_of[6], (4 * D1, D2), (4 * D1) ** -0.5, 0.125),
        "merge_gain": jnp.clip(1.0 + 0.1 * jax.random.normal(streams_of[7], (D2,), jnp.float32), 0.5, 1.5),
        "merge_offset": gaussian(streams_of[8], (D2,), 0.3, 1.5, (), jnp.float32),
        "packed_second": gaussian(streams_of[9], (D2, 3 * HEADS2 * HD), D2 ** -0.5, 0.1875),
        "scale_second": jnp.clip(jnp.exp(jax.random.uniform(streams_of[10], (HEADS2,), jnp.float32, math.log(2.0), math.log(16.0))), 2.0, 16.0),
        "output_second": gaussian(streams_of[11], (HEADS2 * HD, D2), (HEADS2 * HD) ** -0.5, 0.25),
        "gain_second": jnp.clip(1.0 + 0.1 * jax.random.normal(streams_of[12], (D2,), jnp.float32), 0.5, 1.5),
        "offset_second": gaussian(streams_of[13], (D2,), 0.3, 1.5, (), jnp.float32),
    }


norm_eps = 1e-05
unit_eps = 1e-06

def layer_norm(values, norm_gain, offset):
    average = lax.optimization_barrier(jnp.mean(values, axis=-1, keepdims=True))
    centred = values - average
    spread = lax.optimization_barrier(jnp.mean(centred * centred, axis=-1, keepdims=True))
    return centred * lax.rsqrt(spread + norm_eps) * norm_gain + offset

def unit_heads(tensor_in, head_count):
    shaped = tensor_in.astype(jnp.float32).reshape(tensor_in.shape[:-1] + (head_count, tensor_in.shape[-1] // head_count))
    scaled = shaped * lax.rsqrt(lax.optimization_barrier(jnp.sum(shaped * shaped, axis=-1, keepdims=True)) + unit_eps)
    return lax.optimization_barrier(scaled.astype(jnp.bfloat16)).astype(jnp.float32)

def attend(queries, keys_in, values_in, query_region, key_region, scales):
    head_count = scales.shape[0]
    query_unit = unit_heads(queries, head_count)
    key_unit = unit_heads(keys_in, head_count)
    scores = jnp.einsum('nahd,nbhd->nhab', query_unit, key_unit) * scales[None, :, None, None]
    allowed = (query_region[:, :, None] == key_region[:, None, :])[:, None]
    weights = jnp.where(allowed, jnp.exp(scores), jnp.zeros_like(scores))
    totals = lax.optimization_barrier(jnp.sum(weights, axis=-1))
    value_heads = values_in.astype(jnp.float32).reshape(values_in.shape[:-1] + (head_count, values_in.shape[-1] // head_count))
    rounded = lax.optimization_barrier(weights.astype(jnp.bfloat16)).astype(jnp.float32)
    mixture = jnp.einsum('nhab,nbhd->nahd', rounded, value_heads)
    mixture = mixture / jnp.transpose(totals, (0, 2, 1))[..., None]
    return mixture.reshape(queries.shape).astype(jnp.bfloat16)

def shifted_block(features, packed, scales, output_weight, norm_gain, offset):
    levels, row_count, col_count, channels = features.shape
    inner_width = packed.shape[1] // 3
    rolled = jnp.roll(features, (-(WLEV // 2), -(WLAT // 2), -(WLON // 2)), axis=(0, 1, 2))
    level_wrap = (jnp.arange(levels) >= levels - WLEV // 2).astype(jnp.int32)
    row_wrap = (jnp.arange(row_count) >= row_count - WLAT // 2).astype(jnp.int32)
    region = 2 * row_wrap[None, :] + level_wrap[:, None]
    region = jnp.broadcast_to(region[:, :, None], (levels, row_count, col_count))
    window_shape = (levels // WLEV, WLEV, row_count // WLAT, WLAT, col_count // WLON, WLON)
    axis_order = (2, 0, 4, 1, 3, 5)
    tokens = jnp.transpose(rolled.reshape(window_shape + (channels,)), axis_order + (6,))
    tokens = tokens.reshape(row_count // WLAT, levels // WLEV * (col_count // WLON), WLEV * WLAT * WLON, channels)
    regions = jnp.transpose(region.reshape(window_shape), axis_order).reshape(tokens.shape[:3])

    def one_band(pair_items):
        band_tokens, band_region = pair_items
        packed_rows = jnp.dot(band_tokens.reshape(-1, channels), packed, preferred_element_type=jnp.float32).astype(jnp.bfloat16)
        packed_rows = packed_rows.reshape(band_tokens.shape[0], band_tokens.shape[1], 3 * inner_width)
        context = attend(packed_rows[..., :inner_width], packed_rows[..., inner_width:2 * inner_width], packed_rows[..., 2 * inner_width:], band_region, band_region, scales)
        projected = jnp.dot(context.reshape(-1, inner_width), output_weight, preferred_element_type=jnp.float32)
        return layer_norm(projected, norm_gain, offset).reshape(band_tokens.shape[0], band_tokens.shape[1], -1)
    branch = lax.map(one_band, (tokens, regions))
    out_channels = branch.shape[-1]
    branch = branch.reshape((row_count // WLAT, levels // WLEV, col_count // WLON, WLEV, WLAT, WLON, out_channels))
    branch = jnp.transpose(branch, (1, 3, 0, 4, 2, 5, 6)).reshape(levels, row_count, col_count, out_channels)
    branch = jnp.roll(branch, (WLEV // 2, WLAT // 2, WLON // 2), axis=(0, 1, 2))
    return (features.astype(jnp.float32) + branch).astype(jnp.bfloat16)

def reference(features, packed_first, scale_first, output_first, gain_first, offset_first, merge_weight, merge_gain, merge_offset, packed_second, scale_second, output_second, gain_second, offset_second):
    first_out = shifted_block(features, packed_first, scale_first, output_first, gain_first, offset_first)
    levels, row_count, col_count, channels = first_out.shape
    merge_parts = first_out.reshape(levels, row_count // 2, 2, col_count // 2, 2, channels)
    merge_parts = jnp.transpose(merge_parts, (0, 1, 3, 4, 2, 5)).reshape(-1, 4 * channels)
    merged = layer_norm(jnp.dot(merge_parts, merge_weight, preferred_element_type=jnp.float32), merge_gain, merge_offset)
    merged = merged.astype(jnp.bfloat16).reshape(levels, row_count // 2, col_count // 2, -1)
    second = shifted_block(merged, packed_second, scale_second, output_second, gain_second, offset_second)
    wide_channels = second.shape[-1]
    blocks = col_count // 2 // WLON
    second = second.reshape(2, levels // 2, row_count // 2, blocks, WLON, wide_channels)
    second = jnp.transpose(second, (2, 3, 0, 1, 4, 5))
    return second.reshape(row_count // 2, 2 * blocks, levels // 2, WLON, wide_channels)
```

```python
import functools
import math

import jax
import jax.numpy as jnp
import numpy as np
from jax import lax
from jax.experimental import pallas as pl
from jax.experimental.pallas import tpu as pltpu
from jax.sharding import PartitionSpec as P

WLEV = 2
WLAT = 6
WLON = 12
HALF_LAT = WLAT // 2
HALF_LON = WLON // 2
LANES = 128
SHUT = -30000.0

norm_eps = 1e-05
unit_eps = 1e-06

PART = WLEV * HALF_LAT * HALF_LON
GROUP = -(-2 * PART // 16) * 16


def rolled_levels(levels):
    return [(l + WLEV // 2) % levels for l in range(levels)]


def window_slots(levels):
    order = rolled_levels(levels)
    for place, level in enumerate(order):
        pair, lev = divmod(place, WLEV)
        for side in range(2):
            for i in range(HALF_LAT):
                for c in range(HALF_LON):
                    t = (i * WLEV + lev) * HALF_LON + c
                    yield pair * GROUP + side * PART + t, side, level, i, c


def slot_table(levels):
    table = {}
    for row, side, level, i, c in window_slots(levels):
        table[(side, level, i, c)] = row
    return table


def column(values):
    return np.asarray(values, np.int32).reshape(-1, 1)


def fine_gather(levels):
    rows = levels // WLEV * GROUP
    out = [np.full(rows, -1), np.full(rows, -1)]
    for row, side, level, i, c in window_slots(levels):
        out[side][row] = (i * levels + level) * HALF_LON + c
    return column(out[0]), column(out[1])


def patch_gather(levels, row_count):
    span = levels // WLEV * GROUP
    slots = slot_table(levels)
    out = []
    for g in range(4):
        dc, dr = divmod(g, 2)
        rows = []
        for i in range(row_count // 2):
            for level in range(levels):
                for cc in range(HALF_LON // 2):
                    r = 2 * i + dr
                    chunk = r // HALF_LAT + 1
                    w, side = divmod(chunk, 2)
                    rows.append(w * span + slots[(side, level, r % HALF_LAT, 2 * cc + dc)])
        out.append(column(rows))
    return np.stack(out)


def coarse_gather(levels, row_count):
    span = levels // WLEV * GROUP
    chunks = row_count // HALF_LAT
    windows = (chunks + 2) // 2
    third = HALF_LON // 2
    small = HALF_LAT * levels * third
    out = np.full((3, windows * span, 1), -1, np.int32)
    for w in range(windows):
        for row, side, level, i, c in window_slots(levels):
            chunk = 2 * w + side - 1
            which, cc = divmod(c, third)
            cell = (i * levels + level) * third + cc
            at = w * span + row
            if 0 <= chunk < chunks:
                out[which, at, 0] = chunk * small + cell
            else:
                out[2, at, 0] = (0 if chunk < 0 else 2 * small) + which * small + cell
    return out


def edge_gather(levels, row_count):
    third = HALF_LON // 2
    small = HALF_LAT * levels * third
    chunks = row_count // HALF_LAT
    out = np.full((2, 2, 2 * small, 1), -1, np.int32)
    for end in range(2):
        base = 0 if end == 0 else (chunks - 1) * small
        for which in range(2):
            out[end, which, which * small : (which + 1) * small, 0] = base + np.arange(small)
    return out


def final_gather(levels, row_count, even):
    span = levels // WLEV * GROUP
    slots = slot_table(levels)
    third = HALF_LON // 2
    halves = []
    for part in range(2):
        h = part if even else 1 - part
        rows = []
        for r in range(row_count):
            for e in range(levels // 2):
                for c in range(HALF_LON):
                    place = (c + third) % HALF_LON if even else c
                    w, side = divmod(r // HALF_LAT + 1, 2)
                    level = h * (levels // 2) + e
                    rows.append(w * span + slots[(side, level, r % HALF_LAT, place)])
        halves.append(column(rows))
    return np.stack(halves)


def aux_tables(levels):
    pairs = levels // WLEV
    order = rolled_levels(levels)
    hot = np.zeros((2, GROUP, LANES), np.float32)
    shut = np.zeros((pairs, 2, 2, GROUP, LANES), np.float32)
    sides = np.arange(GROUP) // PART
    levs = np.arange(GROUP) % PART // HALF_LON % WLEV
    valid = np.arange(GROUP) < 2 * PART
    for half in range(2):
        base = LANES // 2 * (1 - half)
        for side in range(2):
            for lev in range(WLEV):
                lane = base + side * WLEV + lev
                member = valid & (sides == side) & (levs == lev)
                if side == 0 and lev == 0:
                    member = member | ~valid
                hot[half, :, lane] = member
                for pair in range(pairs):
                    wrapped = [order[pair * WLEV + v] < WLEV // 2 for v in range(WLEV)]
                    same = np.asarray([wrapped[v] == wrapped[lev] for v in range(WLEV)])[levs]
                    for wrap in range(2):
                        allowed = valid & same
                        if wrap:
                            allowed = allowed & (sides == side)
                        shut[pair, wrap, half, :, lane] = np.where(allowed, 0.0, SHUT)
    return hot, shut


def one_hot(index, width):
    lanes = lax.broadcasted_iota(jnp.int32, (index.shape[0], width), 1)
    return (lanes == index).astype(jnp.float32).astype(jnp.bfloat16)


def mm(a, b):
    return jnp.dot(a, b, preferred_element_type=jnp.float32)


def layer_norm(values, norm_gain, offset):
    average = jnp.mean(values, axis=-1, keepdims=True)
    centred = values - average
    spread = jnp.mean(centred * centred, axis=-1, keepdims=True)
    return centred * lax.rsqrt(spread + norm_eps) * norm_gain + offset


def window_context(own, other, weight_ref, scale, wrap, hot_ref, shut_ref, ctx_ref):
    width = weight_ref.shape[1] // 3
    pairs = own.shape[0] // GROUP
    mine = mm(own, weight_ref[...])
    theirs = mm(other, weight_ref[:, width:])
    rows = lax.broadcasted_iota(jnp.int32, (LANES, LANES), 0) // (LANES // 2)
    cols = lax.broadcasted_iota(jnp.int32, (LANES, LANES), 1) // (LANES // 2)
    same = (rows == cols).astype(jnp.float32).astype(jnp.bfloat16)
    lane = lax.broadcasted_iota(jnp.int32, (1, LANES), 1)
    first = (lane < LANES // 2).astype(jnp.float32)
    keep = [first.astype(jnp.bfloat16), (1.0 - first).astype(jnp.bfloat16)]
    fill = [keep[1], keep[0]]
    is_first = lax.broadcasted_iota(jnp.int32, (GROUP, LANES), 1) < LANES // 2

    def unit(block):
        total = mm((block * block).astype(jnp.bfloat16), same)
        return block * lax.rsqrt(total + unit_eps)

    for j in range(width // LANES):
        at = slice(j * LANES, (j + 1) * LANES)
        q = (unit(mine[:, at]) * scale[:, at]).astype(jnp.bfloat16)
        k_at = slice(width + j * LANES, width + (j + 1) * LANES)
        k_own = unit(mine[:, k_at]).astype(jnp.bfloat16)
        k_other = unit(theirs[:, at]).astype(jnp.bfloat16)
        v_own = mine[:, 2 * width + j * LANES : 2 * width + (j + 1) * LANES].astype(jnp.bfloat16)
        v_other = theirs[:, k_at].astype(jnp.bfloat16)
        for pair in range(pairs):
            part = slice(pair * GROUP, (pair + 1) * GROUP)
            out = []
            for half in range(2):
                shut = shut_ref[pair, wrap, half]
                qh = q[part] * keep[half] + hot_ref[half]
                kh = jnp.concatenate(
                    [k_own[part] * keep[half] + shut, k_other[part] * keep[half] + shut], axis=0
                )
                vh = jnp.concatenate(
                    [v_own[part] * keep[half] + fill[half], v_other[part] * keep[half] + fill[half]],
                    axis=0,
                )
                score = lax.dot_general(
                    qh, kh, (((1,), (1,)), ((), ())), preferred_element_type=jnp.float32
                )
                out.append(mm(jnp.exp2(score).astype(jnp.bfloat16), vh))
            top = jnp.where(is_first, out[0], out[1])
            total = pltpu.roll(jnp.where(is_first, out[1], out[0]), LANES // 2, 1)
            ctx_ref[part, at] = (top / total).astype(jnp.bfloat16)


def side_kernel(
    with_edges,
    flags,
    own_ref,
    other_ref,
    own_rim_ref,
    other_rim_ref,
    packed_ref,
    scale_ref,
    output_ref,
    gain_ref,
    offset_ref,
    merge_ref,
    merge_gain_ref,
    merge_offset_ref,
    hot_ref,
    shut_ref,
    index_a_ref,
    index_b_ref,
    patch_ref,
    *rest,
):
    if with_edges:
        near_ref, edge_ref, merged_ref, up_ref, down_ref, own, other, ctx_ref, first_ref = rest
    else:
        merged_ref, own, other, ctx_ref, first_ref = rest
    chunks = own_ref.shape[0]
    for dst, src, rim in ((own, own_ref, own_rim_ref), (other, other_ref, other_rim_ref)):
        dst[0] = rim[0]
        dst[1 : chunks + 1] = src[...]
        dst[chunks + 1] = rim[1]
    windows = (chunks + 2) // 2
    tokens = own_ref.shape[1]
    pick_a = one_hot(index_a_ref[...], tokens)
    pick_b = one_hot(index_b_ref[...], tokens)

    @pl.loop(0, windows)
    def _(w):
        wrap = jnp.where(w == 0, flags[0], jnp.where(w == windows - 1, flags[1], 0))
        mine = mm(pick_a, own[2 * w]) + mm(pick_b, own[2 * w + 1])
        theirs = mm(pick_a, other[2 * w]) + mm(pick_b, other[2 * w + 1])
        window_context(
            mine.astype(jnp.bfloat16),
            theirs.astype(jnp.bfloat16),
            packed_ref,
            scale_ref[...],
            wrap,
            hot_ref,
            shut_ref,
            ctx_ref,
        )
        branch = layer_norm(mm(ctx_ref[...], output_ref[...]), gain_ref[...], offset_ref[...])
        first_ref[w] = (mine + branch).astype(jnp.bfloat16)

    first = first_ref[...].reshape(-1, first_ref.shape[-1])
    channels = first.shape[1]
    total = None
    for g in range(4):
        part = mm(one_hot(patch_ref[g], first.shape[0]), first).astype(jnp.bfloat16)
        term = mm(part, merge_ref[g * channels : (g + 1) * channels])
        total = term if total is None else total + term
    merged = layer_norm(total, merge_gain_ref[...], merge_offset_ref[...]).astype(jnp.bfloat16)
    merged_ref[...] = merged
    if with_edges:
        for end, dst in ((0, up_ref), (1, down_ref)):
            dst[...] = (
                mm(one_hot(edge_ref[end, 0], merged.shape[0]), near_ref[...])
                + mm(one_hot(edge_ref[end, 1], merged.shape[0]), merged)
            ).astype(jnp.bfloat16)


def second_kernel(
    flags,
    near_ref,
    far_ref,
    rim_ref,
    other_near_ref,
    other_far_ref,
    other_rim_ref,
    packed_ref,
    scale_ref,
    output_ref,
    gain_ref,
    offset_ref,
    hot_ref,
    shut_ref,
    coarse_ref,
    final_ref,
    keep_ref,
    send_ref,
    ctx_ref,
    second_ref,
):
    windows, span, _ = second_ref.shape

    @pl.loop(0, windows)
    def _(w):
        wrap = jnp.where(w == 0, flags[0], jnp.where(w == windows - 1, flags[1], 0))
        rows = pl.ds(pl.multiple_of(w * span, 8), span)
        pick = [one_hot(coarse_ref[s, rows], near_ref.shape[0]) for s in range(3)]
        mine = mm(pick[0], near_ref[...]) + mm(pick[1], far_ref[...]) + mm(pick[2], rim_ref[...])
        theirs = (
            mm(pick[0], other_near_ref[...])
            + mm(pick[1], other_far_ref[...])
            + mm(pick[2], other_rim_ref[...])
        )
        window_context(
            mine.astype(jnp.bfloat16),
            theirs.astype(jnp.bfloat16),
            packed_ref,
            scale_ref[...],
            wrap,
            hot_ref,
            shut_ref,
            ctx_ref,
        )
        branch = layer_norm(mm(ctx_ref[...], output_ref[...]), gain_ref[...], offset_ref[...])
        second_ref[w] = (mine + branch).astype(jnp.bfloat16)

    second = second_ref[...].reshape(windows * span, -1)
    keep_ref[...] = mm(one_hot(final_ref[0], windows * span), second).astype(jnp.bfloat16)
    send_ref[...] = mm(one_hot(final_ref[1], windows * span), second).astype(jnp.bfloat16)


def call(kernel, outs, scratch, operands):
    vmem = pl.BlockSpec(memory_space=pltpu.VMEM)
    return pl.pallas_call(
        kernel,
        out_shape=outs,
        in_specs=[pl.BlockSpec(memory_space=pltpu.SMEM)] + [vmem] * (len(operands) - 1),
        out_specs=[vmem] * len(outs),
        scratch_shapes=scratch,
    )(*operands)


def near_swap(value):
    return lax.ppermute(value, "lon", [(i, i ^ 1) for i in range(lax.axis_size("lon"))])


def far_swap(value):
    n = lax.axis_size("lon")
    return lax.ppermute(value, "lon", [(i, (i + (1 if i % 2 else -1)) % n) for i in range(n)])


def up(value):
    return lax.ppermute(value, "lat", [(i, i - 1) for i in range(1, lax.axis_size("lat"))])


def down(value):
    return lax.ppermute(value, "lat", [(i, i + 1) for i in range(lax.axis_size("lat") - 1)])


def lane_scale(scales, head):
    return jnp.repeat(scales * math.log2(math.e), head)[None]


def body(
    features,
    packed_first,
    scale_first,
    output_first,
    gain_first,
    offset_first,
    merge_weight,
    merge_gain,
    merge_offset,
    packed_second,
    scale_second,
    output_second,
    gain_second,
    offset_second,
):
    levels, row_count, col_count, channels = features.shape
    inner = packed_first.shape[1] // 3
    second_inner = packed_second.shape[1] // 3
    wide = merge_weight.shape[1]
    half_rows = row_count // 2
    lat_pos = lax.axis_index("lat")
    is_even = lax.axis_index("lon") % 2 == 0
    flags = jnp.stack([lat_pos == 0, lat_pos == lax.axis_size("lat") - 1]).astype(jnp.int32)
    bf16 = jnp.bfloat16
    span = levels // WLEV * GROUP
    tokens = HALF_LAT * levels * HALF_LON
    chunks = row_count // HALF_LAT

    turned = jnp.transpose(features, (1, 0, 2, 3))
    left, right = turned[:, :, :HALF_LON], turned[:, :, HALF_LON:]
    near = jnp.where(is_even, right, left).reshape(chunks, tokens, channels)
    far = jnp.where(is_even, left, right).reshape(chunks, tokens, channels)

    far_other = far_swap(far)
    near_other = near_swap(near)
    bottom = up(jnp.stack([near[0], far[0]]))
    top = down(jnp.stack([near[-1], far[-1]]))
    near_rim = jnp.stack([top[0], bottom[0]])
    far_rim = jnp.stack([top[1], bottom[1]])
    near_other_rim = near_swap(near_rim)
    far_other_rim = far_swap(far_rim)

    hot, shut = aux_tables(levels)
    hot, shut = jnp.asarray(hot, bf16), jnp.asarray(shut, bf16)
    index_a, index_b = fine_gather(levels)
    head = inner // scale_first.shape[0]
    shared = [
        packed_first,
        lane_scale(scale_first, head),
        output_first,
        gain_first[None],
        offset_first[None],
        merge_weight,
        merge_gain[None],
        merge_offset[None],
        hot,
        shut,
        jnp.asarray(index_a),
        jnp.asarray(index_b),
        jnp.asarray(patch_gather(levels, row_count)),
    ]
    cells = half_rows * levels * HALF_LON // 2
    small = jax.ShapeDtypeStruct((cells, wide), bf16)
    edge = jax.ShapeDtypeStruct((HALF_LAT * levels * HALF_LON, wide), bf16)
    scratch = [
        pltpu.VMEM((chunks + 2, tokens, channels), bf16),
        pltpu.VMEM((chunks + 2, tokens, channels), bf16),
        pltpu.VMEM((span, inner), bf16),
        pltpu.VMEM(((chunks + 2) // 2, span, channels), bf16),
    ]
    (merged_near,) = call(
        functools.partial(side_kernel, False),
        [small],
        scratch,
        [flags, near, near_other, near_rim, near_other_rim] + shared,
    )
    merged_far, edge_up, edge_down = call(
        functools.partial(side_kernel, True),
        [small, edge, edge],
        scratch,
        [flags, far, far_other, far_rim, far_other_rim]
        + shared
        + [merged_near, jnp.asarray(edge_gather(levels, half_rows))],
    )
    other_near = far_swap(merged_near)
    other_far = far_swap(merged_far)
    bottom = up(edge_up)
    top = down(edge_down)
    rim = jnp.concatenate([top, bottom])
    other_rim = far_swap(rim)

    finals = jnp.where(
        is_even,
        jnp.asarray(final_gather(levels, half_rows, True)),
        jnp.asarray(final_gather(levels, half_rows, False)),
    )
    windows = (half_rows // HALF_LAT + 2) // 2
    share = jax.ShapeDtypeStruct((half_rows * levels // 2 * HALF_LON, wide), bf16)
    keep, send = call(
        second_kernel,
        [share, share],
        [pltpu.VMEM((span, second_inner), bf16), pltpu.VMEM((windows, span, wide), bf16)],
        [
            flags,
            merged_near,
            merged_far,
            rim,
            other_near,
            other_far,
            other_rim,
            packed_second,
            lane_scale(scale_second, second_inner // scale_second.shape[0]),
            output_second,
            gain_second[None],
            offset_second[None],
            hot,
            shut,
            jnp.asarray(coarse_gather(levels, half_rows)),
            finals,
        ],
    )
    received = near_swap(send)
    shape = (half_rows, levels // 2, HALF_LON, wide)
    keep, received = keep.reshape(shape), received.reshape(shape)
    out = jnp.where(
        is_even,
        jnp.concatenate([keep, received], axis=2),
        jnp.concatenate([received, keep], axis=2),
    )
    return out[:, None]


def solution(mesh):
    return jax.shard_map(
        body,
        mesh=mesh,
        in_specs=(P(None, "lat", "lon", None),) + (P(),) * 13,
        out_specs=P("lat", "lon", None, None, None),
        check_vma=False,
    )
```

```python
import math

import jax
import jax.numpy as jnp
import numpy as np
from jax import lax
from jax.experimental import pallas as pl
from jax.experimental.pallas import tpu as pltpu
from jax.sharding import PartitionSpec as P

WLEV = 2
WLAT = 6
WLON = 12
HALF_LAT = WLAT // 2
HALF_LON = WLON // 2
LANES = 128

norm_eps = 1e-05
unit_eps = 1e-06

PART = WLEV * HALF_LAT * HALF_LON
GROUP = -(-2 * PART // 16) * 16


def rolled_levels(levels):
    return [(l + WLEV // 2) % levels for l in range(levels)]


def window_slots(levels):
    order = rolled_levels(levels)
    for place, level in enumerate(order):
        pair, lev = divmod(place, WLEV)
        for side in range(2):
            for i in range(HALF_LAT):
                for c in range(HALF_LON):
                    t = (i * WLEV + lev) * HALF_LON + c
                    yield pair * GROUP + side * PART + t, side, level, i, c


def slot_table(levels):
    table = {}
    for row, side, level, i, c in window_slots(levels):
        table[(side, level, i, c)] = row
    return table


def column(values):
    return np.asarray(values, np.int32).reshape(-1, 1)


def fine_gather(levels):
    rows = levels // WLEV * GROUP
    out = [np.full(rows, -1), np.full(rows, -1)]
    for row, side, level, i, c in window_slots(levels):
        out[side][row] = (i * levels + level) * HALF_LON + c
    return column(out[0]), column(out[1])


def patch_gather(levels, row_count):
    span = levels // WLEV * GROUP
    slots = slot_table(levels)
    out = []
    for g in range(4):
        dc, dr = divmod(g, 2)
        rows = []
        for i in range(row_count // 2):
            for level in range(levels):
                for cc in range(HALF_LON // 2):
                    r = 2 * i + dr
                    chunk = r // HALF_LAT + 1
                    w, side = divmod(chunk, 2)
                    rows.append(w * span + slots[(side, level, r % HALF_LAT, 2 * cc + dc)])
        out.append(column(rows))
    return np.concatenate(out)


def coarse_gather(levels, row_count):
    span = levels // WLEV * GROUP
    chunks = row_count // HALF_LAT
    third = HALF_LON // 2
    small = HALF_LAT * levels * third
    out = np.full((3, chunks // 2 * span, 1), -(1 << 20), np.int32)
    for w in range(chunks // 2):
        for row, side, level, i, c in window_slots(levels):
            chunk = 2 * w + side + 1
            which, cc = divmod(c, third)
            cell = (i * levels + level) * third + cc
            at = w * span + row
            if chunk < chunks:
                low = coarse_reach(w, small, chunks * small)[0]
                out[which, at, 0] = chunk * small + cell - low
            else:
                out[2, at, 0] = which * small + cell
    return out


def coarse_reach(w, small, count):
    return (2 * w + 1) * small // 16 * 16, min(padded((2 * w + 3) * small), count)


def edge_gather(levels):
    small = HALF_LAT * levels * HALF_LON // 2
    out = np.full((2, 2 * small, 1), -1, np.int32)
    for which in range(2):
        out[which, which * small : (which + 1) * small, 0] = np.arange(small)
    return out


def coarse_slot(levels, even, r, level, c):
    third = HALF_LON // 2
    place = (c + third) % HALF_LON if even else c
    w, side = divmod(r // HALF_LAT - 1, 2)
    return w * (levels // WLEV * GROUP) + slot_table(levels)[(side, level, r % HALF_LAT, place)]


def padded(count):
    return -(-count // 16) * 16


def send_gather(levels, row_count, even):
    half = levels // 2
    mine, theirs = (0, half) if even else (half, 0)
    parts = []
    for base, low, high in (
        (theirs, HALF_LAT, row_count),
        (mine, row_count, row_count + HALF_LAT),
        (theirs, row_count, row_count + HALF_LAT),
    ):
        rows = [
            coarse_slot(levels, even, r, base + e, c)
            for r in range(low, high)
            for e in range(half)
            for c in range(HALF_LON)
        ]
        parts += rows + [-1] * (padded(len(rows)) - len(rows))
    return column(parts)


def place_gather(levels, row_count, even):
    half = levels // 2
    out = np.full((4, row_count, WLON, half), -1)
    base = 0 if even else half
    for r in range(row_count):
        for e in range(half):
            for c in range(HALF_LON):
                mine, theirs = (c, c + HALF_LON) if even else (c + HALF_LON, c)
                if r >= HALF_LAT:
                    out[0, r, mine, e] = coarse_slot(levels, even, r, base + e, c)
                    out[1, r, theirs, e] = ((r - HALF_LAT) * half + e) * HALF_LON + c
                else:
                    out[2, r, mine, e] = (r * half + e) * HALF_LON + c
                    out[3, r, theirs, e] = (r * half + e) * HALF_LON + c
    return out.reshape(4, -1, 1).astype(np.int32)


def open_tables(levels):
    order = rolled_levels(levels)
    sides = np.arange(GROUP) // PART
    levs = np.arange(GROUP) % PART // HALF_LON % WLEV
    valid = np.arange(GROUP) < 2 * PART
    out = np.zeros((levels // WLEV, 2, GROUP, GROUP), np.float32)
    for pair in range(levels // WLEV):
        wrapped = np.asarray([order[pair * WLEV + v] < WLEV // 2 for v in range(WLEV)])[levs]
        seen = (wrapped[:, None] == wrapped[None]) & valid[None]
        out[pair, 0] = seen
        out[pair, 1] = seen & ((sides[:, None] == sides[None]) | ~valid[:, None])
    return np.tile(out, (1, 1, 2, 2))


def one_hot(index, width, zero):
    index = jnp.asarray(index) + zero
    return (index == lax.broadcasted_iota(jnp.int32, (1, width), 1)).astype(jnp.bfloat16)


def mm(a, b):
    return jnp.dot(a, b, preferred_element_type=jnp.float32)


def layer_norm(values, norm_gain, offset):
    average = jnp.mean(values, axis=-1, keepdims=True)
    centred = values - average
    spread = jnp.mean(centred * centred, axis=-1, keepdims=True)
    return centred * lax.rsqrt(spread + norm_eps) * norm_gain + offset


def staged(tasks, stages):
    held = {}
    for step in range(len(tasks) + len(stages) - 1):
        for depth, stage in enumerate(stages):
            at = step - depth
            if 0 <= at < len(tasks):
                held[at] = stage(tasks[at], held.get(at))


def project(own, other, packed_ref, scale_ref, query, key, value):
    width = packed_ref.shape[1] // 3
    block = 2 * LANES
    rows = lax.broadcasted_iota(jnp.int32, (block, block), 0) // (LANES // 2)
    cols = lax.broadcasted_iota(jnp.int32, (block, block), 1) // (LANES // 2)
    same = (rows == cols).astype(jnp.float32).astype(jnp.bfloat16)
    lane = lax.broadcasted_iota(jnp.int32, (1, block), 1)
    first = (lane % LANES < LANES // 2).astype(jnp.float32)
    head = lane // (LANES // 2)
    tasks = []
    for j in range(width // block):
        tasks += [("q", 0, j), ("k", 0, j), ("k", 1, j), ("v", 0, j), ("v", 1, j)]

    def multiply(task, _):
        kind, s, j = task
        start = "qkv".index(kind) * width + j * block
        return mm((own, other)[s][...], packed_ref[:, start : start + block])

    def measure(task, rows):
        if task[0] == "v":
            return rows
        return rows, mm((rows * rows).astype(jnp.bfloat16), same)

    def keep(task, held):
        kind, s, j = task
        at = slice(j * block, (j + 1) * block)
        if kind == "v":
            value[s, :, at] = held.astype(jnp.bfloat16)
            return
        rows, total = held
        rows = rows * lax.rsqrt(total + unit_eps)
        if kind == "k":
            key[s, :, at] = rows.astype(jnp.bfloat16)
            return
        scale = jnp.zeros((1, block), jnp.float32)
        for h in range(2 * block // LANES):
            scale = jnp.where(head == h, scale_ref[j * 2 * block // LANES + h], scale)
        scale = scale * math.log2(math.e)
        query[0, :, at] = (rows * (scale * first)).astype(jnp.bfloat16)
        query[1, :, at] = (rows * (scale * (1.0 - first))).astype(jnp.bfloat16)

    staged(tasks, [multiply, measure, keep])


def attend(wraps, query, key, value, open_ref, prob, ctx):
    width = query.shape[2]
    windows = len(wraps)
    pairs = query.shape[1] // windows // GROUP
    is_first = lax.broadcasted_iota(jnp.int32, (GROUP, LANES), 1) < LANES // 2
    ones = jnp.ones((2 * GROUP, LANES), jnp.bfloat16)
    tasks = [
        (w, pair, slice(j * LANES, (j + 1) * LANES))
        for w in range(windows)
        for pair in range(pairs)
        for j in range(width // LANES)
    ]
    slots = {task[:2] + (task[2].start,): u % prob.shape[0] for u, task in enumerate(tasks)}

    def place(task):
        w, pair, at = task
        base = (w * pairs + pair) * GROUP
        return slice(base, base + GROUP), at, slots[(w, pair, at.start)]

    def score(task, _):
        rows, at, slot = place(task)
        wrap = 0 if wraps[task[0]] is None else wraps[task[0]]
        q = jnp.concatenate([query[0, rows, at], query[1, rows, at]], axis=0)
        k = jnp.concatenate([key[0, rows, at], key[1, rows, at]], axis=0)
        raw = lax.dot_general(q, k, (((1,), (1,)), ((), ())), preferred_element_type=jnp.float32)
        prob[slot] = jnp.exp2(raw).astype(jnp.bfloat16) * open_ref[task[1], wrap]

    def wait(task, _):
        return None

    def mix(task, _):
        rows, at, slot = place(task)
        v = jnp.concatenate([value[0, rows, at], value[1, rows, at]], axis=0)
        out = mm(prob[slot], jnp.concatenate([v, ones], axis=1))
        top = jnp.where(is_first, out[:GROUP, :LANES], out[GROUP:, :LANES])
        total = jnp.where(is_first, out[:GROUP, LANES:], out[GROUP:, LANES:])
        ctx[rows, at] = (top / total).astype(jnp.bfloat16)

    staged(tasks, [score, wait, mix])


def attention_scratch(rows, width):
    bf16 = jnp.bfloat16
    return [
        pltpu.VMEM((2, rows, width), bf16),
        pltpu.VMEM((2, rows, width), bf16),
        pltpu.VMEM((2, rows, width), bf16),
        pltpu.VMEM((8, 2 * GROUP, 2 * GROUP), bf16),
        pltpu.VMEM((rows, width), bf16),
    ]


def fill_windows(dst, pick, sources):
    span = dst.shape[0] // len(sources)
    for w, chunks in enumerate(sources):
        rows = sum(mm(p, chunk) for p, chunk in zip(pick, chunks))
        dst[w * span : (w + 1) * span] = rows.astype(jnp.bfloat16)


def block_rows(own, ctx, output_ref, gain_ref, offset_ref):
    branch = layer_norm(mm(ctx[...], output_ref[...]), gain_ref[...], offset_ref[...])
    return (own[...].astype(jnp.float32) + branch).astype(jnp.bfloat16)


def merge_rows(first, patch_ref, merge_ref, gain_ref, offset_ref):
    cells = patch_ref.shape[0] // 4
    channels = first.shape[1]
    part = mm(patch_ref[...], first[...]).astype(jnp.bfloat16)
    total = None
    for g in range(4):
        term = mm(part[g * cells : (g + 1) * cells], merge_ref[g * channels : (g + 1) * channels])
        total = term if total is None else total + term
    return layer_norm(total, gain_ref[...], offset_ref[...]).astype(jnp.bfloat16)


def side_kernel(
    scale_ref,
    flags,
    own_ref,
    other_ref,
    top_ref,
    bottom_ref,
    other_rim_ref,
    packed_ref,
    output_ref,
    gain_ref,
    offset_ref,
    merge_ref,
    merge_gain_ref,
    merge_offset_ref,
    open_ref,
    pick_ref,
    patch_ref,
    *rest,
):
    if len(rest) == 9:
        side, (merged_ref, *rest) = 0, rest
    else:
        side, (near_ref, edge_ref, merged_ref, up_ref, *rest) = 1, rest
    own, other, query, key, value, prob, ctx, first = rest
    chunks = own_ref.shape[0]
    pick = [pick_ref[0], pick_ref[1]]
    for dst, src, top, bottom in (
        (own, own_ref, top_ref[side], bottom_ref[side]),
        (other, other_ref, other_rim_ref[0], other_rim_ref[1]),
    ):
        line = [top] + [src[e] for e in range(chunks)] + [bottom]
        fill_windows(dst, pick, list(zip(line[::2], line[1::2])))
    project(own, other, packed_ref, scale_ref, query, key, value)
    wraps = [flags[0]] + [None] * (chunks // 2 - 1) + [flags[1]]
    attend(wraps, query, key, value, open_ref, prob, ctx)
    first[...] = block_rows(own, ctx, output_ref, gain_ref, offset_ref)
    merged = merge_rows(first, patch_ref, merge_ref, merge_gain_ref, merge_offset_ref)
    merged_ref[...] = merged
    if side:
        reach = edge_ref.shape[2]
        up_ref[...] = (
            mm(edge_ref[0], near_ref[:reach]) + mm(edge_ref[1], merged[:reach])
        ).astype(jnp.bfloat16)


def second_kernel(
    scale_ref,
    flags,
    near_ref,
    far_ref,
    rim_ref,
    other_near_ref,
    other_far_ref,
    other_rim_ref,
    packed_ref,
    output_ref,
    gain_ref,
    offset_ref,
    open_ref,
    coarse_ref,
    send_at_ref,
    second_ref,
    send_ref,
    return_ref,
    return_near_ref,
    own,
    other,
    query,
    key,
    value,
    prob,
    ctx,
):
    span = open_ref.shape[0] * GROUP
    windows = own.shape[0] // span
    small = rim_ref.shape[0] // 2
    for w in range(windows):
        low, high = coarse_reach(w, small, near_ref.shape[0])
        reach = [(0, low, high), (1, low, high)]
        if w == windows - 1:
            reach.append((2, 0, 2 * small))
        at = slice(w * span, (w + 1) * span)
        mine = theirs = 0.0
        for s, low, high in reach:
            pick = coarse_ref[s, at, : high - low]
            mine += mm(pick, (near_ref, far_ref, rim_ref)[s][low:high])
            theirs += mm(pick, (other_near_ref, other_far_ref, other_rim_ref)[s][low:high])
        own[at] = mine.astype(jnp.bfloat16)
        other[at] = theirs.astype(jnp.bfloat16)
    project(own, other, packed_ref, scale_ref, query, key, value)
    attend([None] * (windows - 1) + [flags[1]], query, key, value, open_ref, prob, ctx)
    second = block_rows(own, ctx, output_ref, gain_ref, offset_ref)
    second_ref[...] = second
    rows = mm(send_at_ref[...], second).astype(jnp.bfloat16)
    at = 0
    for dst in (send_ref, return_ref, return_near_ref):
        count = dst.shape[0]
        dst[...] = rows[at : at + count]
        at += padded(count)


def place_kernel(second_ref, near_ref, back_ref, back_near_ref, a_ref, b_ref, c_ref, out_ref):
    rows, _, columns, pair, _ = out_ref.shape
    step = columns * pair
    edge = HALF_LAT * step
    early = mm(c_ref[0], back_ref[...]) + mm(c_ref[1], back_near_ref[...])
    late = mm(a_ref[...], second_ref[...]) + mm(b_ref[...], near_ref[...])
    for r in range(rows):
        block, base = (early, r * step) if r < HALF_LAT else (late, r * step - edge)
        for c in range(columns):
            out_ref[r, 0, c] = block[base + c * pair : base + (c + 1) * pair].astype(jnp.bfloat16)


def call(kernel, outs, scratch, scalars, operands):
    vmem = pl.BlockSpec(memory_space=pltpu.VMEM)
    return pl.pallas_call(
        kernel,
        out_shape=outs,
        in_specs=[pl.BlockSpec(memory_space=pltpu.SMEM)] * len(scalars) + [vmem] * len(operands),
        out_specs=[vmem] * len(outs),
        scratch_shapes=scratch,
    )(*scalars, *operands)


def far_of(i, n):
    return (i + (1 if i % 2 else -1)) % n


def near_swap(value):
    return lax.ppermute(value, "lon", [(i, i ^ 1) for i in range(lax.axis_size("lon"))])


def far_swap(value):
    n = lax.axis_size("lon")
    return lax.ppermute(value, "lon", [(i, far_of(i, n)) for i in range(n)])


def ring(value, by, turn):
    n, m = lax.axis_size("lat"), lax.axis_size("lon")
    links = [(i * m + j, (i + by) % n * m + turn(j, m)) for i in range(n) for j in range(m)]
    return lax.ppermute(value, ("lat", "lon"), links)


def shift(value, by):
    n = lax.axis_size("lat")
    return lax.ppermute(value, "lat", [(i, i + by) for i in range(n) if 0 <= i + by < n])


def body(
    features,
    packed_first,
    scale_first,
    output_first,
    gain_first,
    offset_first,
    merge_weight,
    merge_gain,
    merge_offset,
    packed_second,
    scale_second,
    output_second,
    gain_second,
    offset_second,
):
    levels, row_count, _, channels = features.shape
    inner = packed_first.shape[1] // 3
    second_inner = packed_second.shape[1] // 3
    wide = merge_weight.shape[1]
    half_rows = row_count // 2
    lat_pos = lax.axis_index("lat")
    odd = lax.axis_index("lon") % 2
    is_even = odd == 0
    last = lax.axis_size("lat") - 1
    place = jnp.stack([lat_pos, lat_pos, 1 - odd])
    flags = (place == jnp.asarray([0, last, 1], jnp.int32)).astype(jnp.int32)
    bf16 = jnp.bfloat16
    span = levels // WLEV * GROUP
    tokens = HALF_LAT * levels * HALF_LON
    chunks = row_count // HALF_LAT
    windows = chunks // 2 + 1

    turned = jnp.transpose(features, (1, 0, 2, 3))
    left, right = turned[:, :, :HALF_LON], turned[:, :, HALF_LON:]
    near = jnp.where(is_even, right, left).reshape(chunks, tokens, channels)
    far = jnp.where(is_even, left, right).reshape(chunks, tokens, channels)

    near_other = near_swap(near)
    bottom = shift(jnp.stack([near[0], far[0]]), -1)
    top = shift(jnp.stack([near[-1], far[-1]]), 1)
    far_other = far_swap(far)
    near_other_rim = near_swap(jnp.stack([top[0], bottom[0]]))
    far_other_rim = far_swap(jnp.stack([top[1], bottom[1]]))

    zero = jnp.minimum(lat_pos, 0)
    opened = jnp.asarray(open_tables(levels), bf16)
    cells = half_rows * levels * HALF_LON // 2
    small = jax.ShapeDtypeStruct((cells, wide), bf16)
    edge = jax.ShapeDtypeStruct((tokens, wide), bf16)

    def scratch(count, width, depth):
        rows = count * span
        return [pltpu.VMEM((rows, depth), bf16)] * 2 + attention_scratch(rows, width)

    shared = [packed_first, output_first, gain_first[None], offset_first[None]]
    shared += [merge_weight, merge_gain[None], merge_offset[None], opened]
    shared += [
        one_hot(np.stack(fine_gather(levels)), tokens, zero),
        one_hot(patch_gather(levels, row_count), windows * span, zero),
    ]
    buffers = scratch(windows, inner, channels) + [pltpu.VMEM((windows * span, channels), bf16)]
    (merged_near,) = call(
        side_kernel,
        [small],
        buffers,
        [scale_first, flags],
        [near, near_other, top, bottom, near_other_rim] + shared,
    )
    other_near = far_swap(merged_near)
    merged_far, edge_up = call(
        side_kernel,
        [small, edge],
        buffers,
        [scale_first, flags],
        [far, far_other, top, bottom, far_other_rim]
        + shared
        + [merged_near, one_hot(edge_gather(levels), padded(tokens // 2), zero)],
    )
    other_far = far_swap(merged_far)
    other_rim = ring(edge_up, -1, far_of)
    rim = ring(edge_up, -1, lambda j, m: j)

    windows = half_rows // WLAT
    share = levels // 2 * HALF_LON

    def chosen(table):
        odd_table, even_table = (jnp.asarray(table(levels, half_rows, e)) for e in (False, True))
        return jnp.where(is_even, even_table, odd_table)

    places = chosen(place_gather)
    start = HALF_LAT * WLON * levels // 2
    back = jax.ShapeDtypeStruct((HALF_LAT * share, wide), bf16)
    second, send, back_same, back_near = call(
        second_kernel,
        [
            jax.ShapeDtypeStruct((windows * span, wide), bf16),
            jax.ShapeDtypeStruct(((half_rows - HALF_LAT) * share, wide), bf16),
            back,
            back,
        ],
        scratch(windows, second_inner, wide),
        [scale_second, flags],
        [
            merged_near,
            merged_far,
            rim,
            other_near,
            other_far,
            other_rim,
            packed_second,
            output_second,
            gain_second[None],
            offset_second[None],
            opened,
            one_hot(coarse_gather(levels, half_rows), padded(tokens), zero),
            one_hot(chosen(send_gather), windows * span, zero),
        ],
    )
    back_near = ring(back_near, 1, lambda j, m: j ^ 1)
    back_same = ring(back_same, 1, lambda j, m: j)
    received = near_swap(send)
    (out,) = call(
        place_kernel,
        [jax.ShapeDtypeStruct((half_rows, 1, WLON, levels // 2, wide), bf16)],
        [],
        [],
        [
            second,
            received,
            back_same,
            back_near,
            one_hot(places[0, start:], second.shape[0], zero),
            one_hot(places[1, start:], received.shape[0], zero),
            one_hot(places[2:, :start], back_same.shape[0], zero),
        ],
    )
    return jnp.transpose(out, (0, 1, 3, 2, 4))


def solution(mesh):
    return jax.shard_map(
        body,
        mesh=mesh,
        in_specs=(P(None, "lat", "lon", None),) + (P(),) * 13,
        out_specs=P("lat", "lon", None, None, None),
        check_vma=False,
    )
```

```python
import math

import jax
import jax.numpy as jnp
import numpy as np
from jax import lax
from jax.experimental import pallas as pl
from jax.experimental.pallas import tpu as pltpu
from jax.sharding import PartitionSpec as P

WLEV = 2
WLAT = 6
WLON = 12
HALF_LAT = WLAT // 2
HALF_LON = WLON // 2
LANES = 128
FIRST_BYTES, SECOND_BYTES = 48 << 20, 32 << 20

norm_eps = 1e-05
unit_eps = 1e-06

PART = WLEV * HALF_LAT * HALF_LON
GROUP = 2 * PART


def rolled_levels(levels):
    return [(l + WLEV // 2) % levels for l in range(levels)]


def window_slots(levels):
    order = rolled_levels(levels)
    for place, level in enumerate(order):
        pair, lev = divmod(place, WLEV)
        for side in range(2):
            for i in range(HALF_LAT):
                for c in range(HALF_LON):
                    t = (i * WLEV + lev) * HALF_LON + c
                    yield pair * GROUP + side * PART + t, side, level, i, c


def slot_table(levels):
    table = {}
    for row, side, level, i, c in window_slots(levels):
        table[(side, level, i, c)] = row
    return table


def column(values):
    return np.asarray(values, np.int32).reshape(-1, 1)


def fine_gather(levels):
    rows = levels // WLEV * GROUP
    out = [np.full(rows, -1), np.full(rows, -1)]
    for row, side, level, i, c in window_slots(levels):
        out[side][row] = (i * levels + level) * HALF_LON + c
    return column(out[0]), column(out[1])


def patch_gather(levels, row_count):
    span = levels // WLEV * GROUP
    slots = slot_table(levels)
    out = []
    for g in range(4):
        dc, dr = divmod(g, 2)
        rows = []
        for i in range(row_count // 2):
            for level in range(levels):
                for cc in range(HALF_LON // 2):
                    r = 2 * i + dr
                    chunk = r // HALF_LAT + 1
                    w, side = divmod(chunk, 2)
                    rows.append(w * span + slots[(side, level, r % HALF_LAT, 2 * cc + dc)])
        out.append(column(rows))
    return np.concatenate(out)


def coarse_gather(levels, row_count):
    span = levels // WLEV * GROUP
    chunks = row_count // HALF_LAT
    third = HALF_LON // 2
    small = HALF_LAT * levels * third
    out = np.full((3, chunks // 2 * span, 1), -(1 << 20), np.int32)
    for w in range(chunks // 2):
        for row, side, level, i, c in window_slots(levels):
            chunk = 2 * w + side + 1
            which, cc = divmod(c, third)
            cell = (i * levels + level) * third + cc
            at = w * span + row
            if chunk < chunks:
                low = coarse_reach(w, small, chunks * small)[0]
                out[which, at, 0] = chunk * small + cell - low
            else:
                out[2, at, 0] = which * small + cell
    return out


def coarse_reach(w, small, count):
    return (2 * w + 1) * small // 16 * 16, min(padded((2 * w + 3) * small), count)


def edge_gather(levels):
    small = HALF_LAT * levels * HALF_LON // 2
    out = np.full((2, 2 * small, 1), -1, np.int32)
    for which in range(2):
        out[which, which * small : (which + 1) * small, 0] = np.arange(small)
    return out


def coarse_slot(levels, even, r, level, c):
    third = HALF_LON // 2
    place = (c + third) % HALF_LON if even else c
    w, side = divmod(r // HALF_LAT - 1, 2)
    return w * (levels // WLEV * GROUP) + slot_table(levels)[(side, level, r % HALF_LAT, place)]


def padded(count):
    return -(-count // 16) * 16


def send_gather(levels, row_count, even):
    half = levels // 2
    mine, theirs = (0, half) if even else (half, 0)
    parts = []
    for base, low, high in (
        (theirs, HALF_LAT, row_count),
        (mine, row_count, row_count + HALF_LAT),
        (theirs, row_count, row_count + HALF_LAT),
    ):
        rows = [
            coarse_slot(levels, even, r, base + e, c)
            for r in range(low, high)
            for e in range(half)
            for c in range(HALF_LON)
        ]
        parts += rows + [-1] * (padded(len(rows)) - len(rows))
    return column(parts)


def place_gather(levels, row_count, even):
    half = levels // 2
    out = np.full((4, row_count, WLON, half), -1)
    base = 0 if even else half
    for r in range(row_count):
        for e in range(half):
            for c in range(HALF_LON):
                mine, theirs = (c, c + HALF_LON) if even else (c + HALF_LON, c)
                if r >= HALF_LAT:
                    out[0, r, mine, e] = coarse_slot(levels, even, r, base + e, c)
                    out[1, r, theirs, e] = ((r - HALF_LAT) * half + e) * HALF_LON + c
                else:
                    out[2, r, mine, e] = (r * half + e) * HALF_LON + c
                    out[3, r, theirs, e] = (r * half + e) * HALF_LON + c
    return out.reshape(4, -1, 1).astype(np.int32)


def open_tables(levels):
    order = rolled_levels(levels)
    sides = np.arange(GROUP) // PART
    levs = np.arange(GROUP) % PART // HALF_LON % WLEV
    out = np.zeros((levels // WLEV, 2, GROUP, GROUP), np.float32)
    for pair in range(levels // WLEV):
        wrapped = np.asarray([order[pair * WLEV + v] < WLEV // 2 for v in range(WLEV)])[levs]
        seen = wrapped[:, None] == wrapped[None]
        out[pair, 0] = seen
        out[pair, 1] = seen & (sides[:, None] == sides[None])
    return np.tile(out, (1, 1, 2, 2))


PATCH, PICK, EDGE, COARSE, SEND, PLACE = 0, 1, 3, 5, 8, 10


def index_table(levels, row_count):
    half_rows = row_count // 2
    columns = [patch_gather(levels, row_count), *fine_gather(levels), *edge_gather(levels)]
    columns += [*coarse_gather(levels, half_rows)]
    columns += [send_gather(levels, half_rows, even) for even in (False, True)]
    for even in (False, True):
        columns += [*place_gather(levels, half_rows, even)]
    out = np.full((padded(max(len(c) for c in columns)), len(columns)), -(1 << 20), np.int32)
    for at, values in enumerate(columns):
        out[: len(values), at] = values[:, 0]
    return out


def column_of(table_ref, at, rows):
    return table_ref[rows, at : at + 1]


def parity_column(table_ref, at, step, even, rows):
    chosen = column_of(table_ref, at + step, rows), column_of(table_ref, at, rows)
    return jnp.where(even == 1, *chosen)


def one_hot(index, width):
    lanes = lax.broadcasted_iota(jnp.int32, (index.shape[0], width), 1)
    return (lanes == index).astype(jnp.float32).astype(jnp.bfloat16)


def mm(a, b):
    return jnp.dot(a, b, preferred_element_type=jnp.float32)


def layer_norm(values, norm_gain, offset):
    average = jnp.mean(values, axis=-1, keepdims=True)
    centred = values - average
    spread = jnp.mean(centred * centred, axis=-1, keepdims=True)
    return centred * lax.rsqrt(spread + norm_eps) * norm_gain + offset


def staged(tasks, stages):
    held = {}
    for step in range(len(tasks) + len(stages) - 1):
        for depth, stage in enumerate(stages):
            at = step - depth
            if 0 <= at < len(tasks):
                held[at] = stage(tasks[at], held.get(at))


def project(own, both, packed_ref, scale_ref, query, key, value):
    width = packed_ref.shape[1] // 3
    block = 2 * LANES
    rows = lax.broadcasted_iota(jnp.int32, (block, block), 0) // (LANES // 2)
    cols = lax.broadcasted_iota(jnp.int32, (block, block), 1) // (LANES // 2)
    same = (rows == cols).astype(jnp.float32).astype(jnp.bfloat16)
    lane = lax.broadcasted_iota(jnp.int32, (1, block), 1)
    first = (lane % LANES < LANES // 2).astype(jnp.float32)
    head = lane // (LANES // 2)
    half = both.shape[0] // 2
    tasks = []
    for j in range(width // block):
        tasks += [("q", 0, j), ("k", 0, j), ("k", 1, j), ("v", 0, j), ("v", 1, j)]

    def multiply(task, _):
        kind, part, j = task
        start = "qkv".index(kind) * width + j * block
        source = own[...] if kind == "q" else both[part * half : (part + 1) * half]
        return mm(source, packed_ref[:, start : start + block])

    def measure(task, rows):
        if task[0] == "v":
            return rows
        return rows, mm((rows * rows).astype(jnp.bfloat16), same)

    def keep(task, held):
        kind, part, j = task
        at = slice(j * block, (j + 1) * block)
        if kind == "v":
            value[part * half : (part + 1) * half, at] = held.astype(jnp.bfloat16)
            return
        rows, total = held
        rows = rows * lax.rsqrt(total + unit_eps)
        if kind == "k":
            key[part * half : (part + 1) * half, at] = rows.astype(jnp.bfloat16)
            return
        scale = jnp.zeros((1, block), jnp.float32)
        for h in range(2 * block // LANES):
            scale = jnp.where(head == h, scale_ref[j * 2 * block // LANES + h], scale)
        scale = scale * math.log2(math.e)
        left, right = rows * (scale * first), rows * (scale * (1.0 - first))
        for g in range(rows.shape[0] // GROUP):
            mine = slice(g * GROUP, (g + 1) * GROUP)
            query[2 * g * GROUP : 2 * (g + 1) * GROUP, at] = jnp.concatenate(
                [left[mine], right[mine]], axis=0
            ).astype(jnp.bfloat16)

    staged(tasks, [multiply, measure, keep])


def attend(wraps, query, key, value, open_ref, prob, ctx):
    width = query.shape[1]
    windows = len(wraps)
    pairs = query.shape[0] // windows // (2 * GROUP)
    is_first = lax.broadcasted_iota(jnp.int32, (GROUP, LANES), 1) < LANES // 2
    ones = jnp.ones((2 * GROUP, LANES), jnp.bfloat16)
    tasks = [
        (w, j, pair) for w in range(windows) for j in range(width // LANES) for pair in range(pairs)
    ]
    done = []

    def place(task):
        w, j, pair = task
        rows = slice((w * pairs + pair) * 2 * GROUP, (w * pairs + pair + 1) * 2 * GROUP)
        return rows, slice(j * LANES, (j + 1) * LANES), tasks.index(task) % prob.shape[0]

    def score(task, _):
        rows, at, slot = place(task)
        wrap, pair = wraps[task[0]], task[2]
        raw = lax.dot_general(
            query[rows, at],
            key[rows, at],
            (((1,), (1,)), ((), ())),
            preferred_element_type=jnp.float32,
        )
        raw = jnp.exp2(raw).astype(jnp.bfloat16)
        if wrap is not None or pair == pairs - 1:
            raw = raw * open_ref[pair, 0 if wrap is None else wrap]
        prob[slot] = raw

    def wait(task, _):
        return None

    def mix(task, _):
        rows, at, slot = place(task)
        out = mm(prob[slot], jnp.concatenate([value[rows, at], ones], axis=1))
        top = jnp.where(is_first, out[:GROUP, :LANES], out[GROUP:, :LANES])
        total = jnp.where(is_first, out[:GROUP, LANES:], out[GROUP:, LANES:])
        done.append(top / total)
        if len(done) == pairs:
            base = task[0] * pairs * GROUP
            ctx[base : base + pairs * GROUP, at] = jnp.concatenate(done, axis=0).astype(jnp.bfloat16)
            done.clear()

    staged(tasks, [score, wait, mix])


def attention_scratch(rows, width, depth):
    bf16 = jnp.bfloat16
    return [
        pltpu.VMEM((rows, depth), bf16),
        pltpu.VMEM((2 * rows, depth), bf16),
        pltpu.VMEM((2 * rows, width), bf16),
        pltpu.VMEM((2 * rows, width), bf16),
        pltpu.VMEM((2 * rows, width), bf16),
        pltpu.VMEM((8, 2 * GROUP, 2 * GROUP), bf16),
        pltpu.VMEM((rows, width), bf16),
    ]


def keep_window(w, mine, theirs, own, both):
    span = mine.shape[0]
    own[w * span : (w + 1) * span] = mine.astype(jnp.bfloat16)
    parts = []
    for at in range(0, span, GROUP):
        parts += [mine[at : at + GROUP], theirs[at : at + GROUP]]
    both[2 * w * span : 2 * (w + 1) * span] = jnp.concatenate(parts, axis=0).astype(jnp.bfloat16)


def block_rows(own, ctx, output_ref, gain_ref, offset_ref):
    branch = layer_norm(mm(ctx[...], output_ref[...]), gain_ref[...], offset_ref[...])
    return (own[...].astype(jnp.float32) + branch).astype(jnp.bfloat16)


def merge_rows(first, patch, merge_ref, gain_ref, offset_ref):
    cells = patch.shape[0] // 4
    channels = first.shape[1]
    part = mm(patch, first[...]).astype(jnp.bfloat16)
    total = None
    for g in range(4):
        term = mm(part[g * cells : (g + 1) * cells], merge_ref[g * channels : (g + 1) * channels])
        total = term if total is None else total + term
    return layer_norm(total, gain_ref[...], offset_ref[...]).astype(jnp.bfloat16)


def side_kernel(
    scale_ref,
    flags,
    own_ref,
    other_ref,
    top_ref,
    bottom_ref,
    other_rim_ref,
    packed_ref,
    output_ref,
    gain_ref,
    offset_ref,
    merge_gain_ref,
    merge_offset_ref,
    open_ref,
    table_ref,
    merge_hbm,
    *rest,
):
    if len(rest) == 11:
        side, (merged_ref, *rest) = 0, rest
    else:
        side, (near_ref, merged_ref, up_ref, *rest) = 1, rest
    merge_ref, sem, first, own, both, query, key, value, prob, ctx = rest
    fetch = pltpu.make_async_copy(merge_hbm, merge_ref, sem)
    fetch.start()
    chunks = own_ref.shape[0]
    tokens = own_ref.shape[1]
    span = open_ref.shape[0] * GROUP
    pick = [one_hot(column_of(table_ref, PICK + s, slice(0, span)), tokens) for s in range(2)]
    lines = []
    for src, top, bottom in (
        (own_ref, top_ref[side], bottom_ref[side]),
        (other_ref, other_rim_ref[0], other_rim_ref[1]),
    ):
        lines.append([top] + [src[e] for e in range(chunks)] + [bottom])
    for w in range(chunks // 2 + 1):
        mine, theirs = (
            mm(pick[0], line[2 * w]) + mm(pick[1], line[2 * w + 1]) for line in lines
        )
        keep_window(w, mine, theirs, own, both)
    project(own, both, packed_ref, scale_ref, query, key, value)
    wraps = [flags[0]] + [None] * (chunks // 2 - 1) + [flags[1]]
    attend(wraps, query, key, value, open_ref, prob, ctx)
    first[...] = block_rows(own, ctx, output_ref, gain_ref, offset_ref)
    fetch.wait()
    cells = 4 * merged_ref.shape[0]
    patch = one_hot(column_of(table_ref, PATCH, slice(0, cells)), first.shape[0])
    merged = merge_rows(first, patch, merge_ref, merge_gain_ref, merge_offset_ref)
    merged_ref[...] = merged
    if side:
        count = up_ref.shape[0]
        reach = padded(count // 2)
        up_ref[...] = sum(
            mm(one_hot(column_of(table_ref, EDGE + s, slice(0, count)), reach), rows[:reach])
            for s, rows in enumerate((near_ref, merged))
        ).astype(jnp.bfloat16)


def second_kernel(
    scale_ref,
    flags,
    near_ref,
    far_ref,
    rim_ref,
    other_near_ref,
    other_far_ref,
    other_rim_ref,
    packed_ref,
    output_ref,
    gain_ref,
    offset_ref,
    open_ref,
    table_ref,
    second_ref,
    send_ref,
    return_ref,
    return_near_ref,
    own,
    both,
    query,
    key,
    value,
    prob,
    ctx,
):
    span = open_ref.shape[0] * GROUP
    windows = own.shape[0] // span
    small = rim_ref.shape[0] // 2
    for w in range(windows):
        low, high = coarse_reach(w, small, near_ref.shape[0])
        reach = [(0, low, high), (1, low, high)]
        if w == windows - 1:
            reach.append((2, 0, 2 * small))
        mine = theirs = 0.0
        for s, low, high in reach:
            at = slice(w * span, (w + 1) * span)
            pick = one_hot(column_of(table_ref, COARSE + s, at), high - low)
            mine += mm(pick, (near_ref, far_ref, rim_ref)[s][low:high])
            theirs += mm(pick, (other_near_ref, other_far_ref, other_rim_ref)[s][low:high])
        keep_window(w, mine, theirs, own, both)
    project(own, both, packed_ref, scale_ref, query, key, value)
    attend([None] * (windows - 1) + [flags[1]], query, key, value, open_ref, prob, ctx)
    second = block_rows(own, ctx, output_ref, gain_ref, offset_ref)
    second_ref[...] = second
    counts = [padded(ref.shape[0]) for ref in (send_ref, return_ref, return_near_ref)]
    index = parity_column(table_ref, SEND, 1, flags[2], slice(0, sum(counts)))
    rows = mm(one_hot(index, second.shape[0]), second).astype(jnp.bfloat16)
    at = 0
    for dst in (send_ref, return_ref, return_near_ref):
        count = dst.shape[0]
        dst[...] = rows[at : at + count]
        at += padded(count)


def place(pieces, out_ref, rows_ref, sem, low):
    rows, _, columns, pair, _ = rows_ref.shape
    block = sum(mm(one_hot(index, ref.shape[0]), ref[...]) for index, ref in pieces)
    for r in range(rows):
        for c in range(columns):
            at = (r * columns + c) * pair
            rows_ref[r, 0, c] = block[at : at + pair].astype(jnp.bfloat16)
    copy = pltpu.make_async_copy(rows_ref, out_ref.at[low : low + rows], sem)
    copy.start()
    copy.wait()


def place_columns(flags, table_ref, out_ref, which, early):
    step = out_ref.shape[2] * out_ref.shape[3]
    edge = HALF_LAT * step
    rows = slice(0, edge) if early else slice(edge, step * out_ref.shape[0])
    return [parity_column(table_ref, PLACE + s, 4, flags[2], rows) for s in which]


def late_kernel(flags, second_ref, near_ref, table_ref, out_ref, rows_ref, sem):
    index = place_columns(flags, table_ref, out_ref, (0, 1), False)
    place(zip(index, (second_ref, near_ref)), out_ref, rows_ref, sem, HALF_LAT)


def early_kernel(flags, back_ref, back_near_ref, table_ref, _, out_ref, rows_ref, sem):
    index = place_columns(flags, table_ref, out_ref, (2, 3), True)
    place(zip(index, (back_ref, back_near_ref)), out_ref, rows_ref, sem, 0)


def call(
    kernel, outs, scratch, scalars, operands, fixed=(), late=(), alias=None, held=False, room=SECOND_BYTES
):
    vmem = pl.BlockSpec(memory_space=pltpu.VMEM)
    hbm = pl.BlockSpec(memory_space=pltpu.HBM)
    return pl.pallas_call(
        kernel,
        out_shape=outs,
        in_specs=[pl.BlockSpec(memory_space=pltpu.SMEM)] * len(scalars)
        + [vmem] * len(operands)
        + [hbm] * len(fixed)
        + [vmem] * len(late),
        out_specs=[hbm if held else vmem] * len(outs),
        scratch_shapes=scratch,
        input_output_aliases=alias or {},
        compiler_params=pltpu.CompilerParams(vmem_limit_bytes=room),
    )(*scalars, *operands, *fixed, *late)


def far_of(i, n):
    return (i + (1 if i % 2 else -1)) % n


def near_swap(value):
    return lax.ppermute(value, "lon", [(i, i ^ 1) for i in range(lax.axis_size("lon"))])


def far_swap(value):
    n = lax.axis_size("lon")
    return lax.ppermute(value, "lon", [(i, far_of(i, n)) for i in range(n)])


def ring(value, by, turn):
    n, m = lax.axis_size("lat"), lax.axis_size("lon")
    links = [(i * m + j, (i + by) % n * m + turn(j, m)) for i in range(n) for j in range(m)]
    return lax.ppermute(value, ("lat", "lon"), links)


def shift(value, by):
    n = lax.axis_size("lat")
    return lax.ppermute(value, "lat", [(i, i + by) for i in range(n) if 0 <= i + by < n])


def body(
    features,
    packed_first,
    scale_first,
    output_first,
    gain_first,
    offset_first,
    merge_weight,
    merge_gain,
    merge_offset,
    packed_second,
    scale_second,
    output_second,
    gain_second,
    offset_second,
):
    levels, row_count, _, channels = features.shape
    inner = packed_first.shape[1] // 3
    second_inner = packed_second.shape[1] // 3
    wide = merge_weight.shape[1]
    half_rows = row_count // 2
    lat_pos = lax.axis_index("lat")
    odd = lax.axis_index("lon") % 2
    is_even = odd == 0
    last = lax.axis_size("lat") - 1
    place = jnp.stack([lat_pos, lat_pos, 1 - odd])
    flags = (place == jnp.asarray([0, last, 1], jnp.int32)).astype(jnp.int32)
    bf16 = jnp.bfloat16
    span = levels // WLEV * GROUP
    tokens = HALF_LAT * levels * HALF_LON
    chunks = row_count // HALF_LAT
    windows = chunks // 2 + 1

    turned = jnp.transpose(features, (1, 0, 2, 3))
    left, right = turned[:, :, :HALF_LON], turned[:, :, HALF_LON:]
    near = jnp.where(is_even, right, left).reshape(chunks, tokens, channels)
    far = jnp.where(is_even, left, right).reshape(chunks, tokens, channels)

    near_other = near_swap(near)
    bottom = shift(jnp.stack([near[0], far[0]]), -1)
    top = shift(jnp.stack([near[-1], far[-1]]), 1)
    far_other = far_swap(far)
    near_other_rim = near_swap(jnp.stack([top[0], bottom[0]]))
    far_other_rim = far_swap(jnp.stack([top[1], bottom[1]]))

    opened = jnp.asarray(open_tables(levels), bf16)
    cells = half_rows * levels * HALF_LON // 2
    small = jax.ShapeDtypeStruct((cells, wide), bf16)
    edge = jax.ShapeDtypeStruct((tokens, wide), bf16)

    shared = [packed_first, output_first, gain_first[None], offset_first[None]]
    shared += [merge_gain[None], merge_offset[None], opened]
    table = jnp.asarray(index_table(levels, row_count))
    shared += [table]
    buffers = [pltpu.VMEM(merge_weight.shape, bf16), pltpu.SemaphoreType.DMA]
    buffers += [pltpu.VMEM((windows * span, channels), bf16)]
    buffers += attention_scratch(windows * span, inner, channels)
    (merged_near,) = call(
        side_kernel,
        [small],
        buffers,
        [scale_first, flags],
        [near, near_other, top, bottom, near_other_rim] + shared,
        [merge_weight],
        room=FIRST_BYTES,
    )
    other_near = far_swap(merged_near)
    merged_far, edge_up = call(
        side_kernel,
        [small, edge],
        buffers,
        [scale_first, flags],
        [far, far_other, top, bottom, far_other_rim] + shared,
        [merge_weight],
        [merged_near],
        room=FIRST_BYTES,
    )
    other_far = far_swap(merged_far)
    other_rim = ring(edge_up, -1, far_of)
    rim = ring(edge_up, -1, lambda j, m: j)

    windows = half_rows // WLAT
    share = levels // 2 * HALF_LON

    back = jax.ShapeDtypeStruct((HALF_LAT * share, wide), bf16)
    second, send, back_same, back_near = call(
        second_kernel,
        [
            jax.ShapeDtypeStruct((windows * span, wide), bf16),
            jax.ShapeDtypeStruct(((half_rows - HALF_LAT) * share, wide), bf16),
            back,
            back,
        ],
        attention_scratch(windows * span, second_inner, wide),
        [scale_second, flags],
        [
            merged_near,
            merged_far,
            rim,
            other_near,
            other_far,
            other_rim,
            packed_second,
            output_second,
            gain_second[None],
            offset_second[None],
            opened,
            table,
        ],
    )
    back_near = ring(back_near, 1, lambda j, m: j ^ 1)
    back_same = ring(back_same, 1, lambda j, m: j)
    received = near_swap(send)
    shape = (half_rows, 1, WLON, levels // 2, wide)
    whole = [jax.ShapeDtypeStruct(shape, bf16)]

    def room(rows):
        return [pltpu.VMEM((rows,) + shape[1:], bf16), pltpu.SemaphoreType.DMA]

    (out,) = call(
        late_kernel,
        whole,
        room(half_rows - HALF_LAT),
        [flags],
        [second, received, table],
        held=True,
    )
    (out,) = call(
        early_kernel,
        whole,
        room(HALF_LAT),
        [flags],
        [back_same, back_near, table],
        [out],
        alias={4: 0},
        held=True,
    )
    return jnp.transpose(out, (0, 1, 3, 2, 4))


def solution(mesh):
    return jax.shard_map(
        body,
        mesh=mesh,
        in_specs=(P(None, "lat", "lon", None),) + (P(),) * 13,
        out_specs=P("lat", "lon", None, None, None),
        check_vma=False,
    )
```

```python
import math

import jax
import jax.numpy as jnp
import numpy as np
from jax import lax
from jax.experimental import pallas as pl
from jax.experimental.pallas import tpu as pltpu
from jax.sharding import PartitionSpec as P

WLEV = 2
WLAT = 6
WLON = 12
HALF_LAT = WLAT // 2
HALF_LON = WLON // 2
LANES = 128
FIRST_BYTES, SECOND_BYTES = 48 << 20, 32 << 20

norm_eps = 1e-05
unit_eps = 1e-06

PART = WLEV * HALF_LAT * HALF_LON
GROUP = 2 * PART


def rolled_levels(levels):
    return [(l + WLEV // 2) % levels for l in range(levels)]


def window_slots(levels):
    order = rolled_levels(levels)
    for place, level in enumerate(order):
        pair, lev = divmod(place, WLEV)
        for side in range(2):
            for i in range(HALF_LAT):
                for c in range(HALF_LON):
                    t = (i * WLEV + lev) * HALF_LON + c
                    yield pair * GROUP + side * PART + t, side, level, i, c


def slot_table(levels):
    table = {}
    for row, side, level, i, c in window_slots(levels):
        table[(side, level, i, c)] = row
    return table


def column(values):
    return np.asarray(values, np.int32).reshape(-1, 1)


def fine_gather(levels):
    rows = levels // WLEV * GROUP
    out = [np.full(rows, -1), np.full(rows, -1)]
    for row, side, level, i, c in window_slots(levels):
        out[side][row] = (i * levels + level) * HALF_LON + c
    return column(out[0]), column(out[1])


def patch_gather(levels, row_count):
    span = levels // WLEV * GROUP
    slots = slot_table(levels)
    out = []
    for g in range(4):
        dc, dr = divmod(g, 2)
        rows = []
        for i in range(row_count // 2):
            for level in range(levels):
                for cc in range(HALF_LON // 2):
                    r = 2 * i + dr
                    chunk = r // HALF_LAT + 1
                    w, side = divmod(chunk, 2)
                    rows.append(w * span + slots[(side, level, r % HALF_LAT, 2 * cc + dc)])
        out.append(column(rows))
    return np.concatenate(out)


def coarse_gather(levels, row_count):
    span = levels // WLEV * GROUP
    chunks = row_count // HALF_LAT
    third = HALF_LON // 2
    small = HALF_LAT * levels * third
    out = np.full((3, chunks // 2 * span, 1), -(1 << 20), np.int32)
    for w in range(chunks // 2):
        for row, side, level, i, c in window_slots(levels):
            chunk = 2 * w + side + 1
            which, cc = divmod(c, third)
            cell = (i * levels + level) * third + cc
            at = w * span + row
            if chunk < chunks:
                low = coarse_reach(w, small, chunks * small)[0]
                out[which, at, 0] = chunk * small + cell - low
            else:
                out[2, at, 0] = which * small + cell
    return out


def coarse_reach(w, small, count):
    return (2 * w + 1) * small // 16 * 16, min(padded((2 * w + 3) * small), count)


def edge_gather(levels):
    small = HALF_LAT * levels * HALF_LON // 2
    out = np.full((2, 2 * small, 1), -1, np.int32)
    for which in range(2):
        out[which, which * small : (which + 1) * small, 0] = np.arange(small)
    return out


def coarse_slot(levels, even, r, level, c):
    third = HALF_LON // 2
    place = (c + third) % HALF_LON if even else c
    w, side = divmod(r // HALF_LAT - 1, 2)
    return w * (levels // WLEV * GROUP) + slot_table(levels)[(side, level, r % HALF_LAT, place)]


def padded(count):
    return -(-count // 16) * 16


def send_gather(levels, row_count, even):
    half = levels // 2
    mine, theirs = (0, half) if even else (half, 0)
    parts = []
    for base, low, high in (
        (theirs, HALF_LAT, row_count),
        (mine, row_count, row_count + HALF_LAT),
        (theirs, row_count, row_count + HALF_LAT),
    ):
        rows = [
            coarse_slot(levels, even, r, base + e, c)
            for r in range(low, high)
            for e in range(half)
            for c in range(HALF_LON)
        ]
        parts += rows + [-1] * (padded(len(rows)) - len(rows))
    return column(parts)


def place_gather(levels, row_count, even):
    half = levels // 2
    out = np.full((4, row_count, WLON, half), -1)
    base = 0 if even else half
    for r in range(row_count):
        for e in range(half):
            for c in range(HALF_LON):
                mine, theirs = (c, c + HALF_LON) if even else (c + HALF_LON, c)
                if r >= HALF_LAT:
                    out[0, r, mine, e] = coarse_slot(levels, even, r, base + e, c)
                    out[1, r, theirs, e] = ((r - HALF_LAT) * half + e) * HALF_LON + c
                else:
                    out[2, r, mine, e] = (r * half + e) * HALF_LON + c
                    out[3, r, theirs, e] = (r * half + e) * HALF_LON + c
    return out.reshape(4, -1, 1).astype(np.int32)


def open_tables(levels):
    order = rolled_levels(levels)
    sides = np.arange(GROUP) // PART
    levs = np.arange(GROUP) % PART // HALF_LON % WLEV
    out = np.zeros((levels // WLEV, 2, GROUP, GROUP), np.float32)
    for pair in range(levels // WLEV):
        wrapped = np.asarray([order[pair * WLEV + v] < WLEV // 2 for v in range(WLEV)])[levs]
        seen = wrapped[:, None] == wrapped[None]
        out[pair, 0] = seen
        out[pair, 1] = seen & (sides[:, None] == sides[None])
    return np.tile(out, (1, 1, 2, 2))


PATCH, PICK, EDGE, COARSE, SEND, PLACE = 0, 1, 3, 5, 8, 10


def index_table(levels, row_count):
    half_rows = row_count // 2
    columns = [patch_gather(levels, row_count), *fine_gather(levels), *edge_gather(levels)]
    columns += [*coarse_gather(levels, half_rows)]
    columns += [send_gather(levels, half_rows, even) for even in (False, True)]
    for even in (False, True):
        columns += [*place_gather(levels, half_rows, even)]
    out = np.full((padded(max(len(c) for c in columns)), len(columns)), -(1 << 20), np.int32)
    for at, values in enumerate(columns):
        out[: len(values), at] = values[:, 0]
    return out


def column_of(table_ref, at, rows):
    return table_ref[rows, at : at + 1]


def parity_column(table_ref, at, step, even, rows):
    chosen = column_of(table_ref, at + step, rows), column_of(table_ref, at, rows)
    return jnp.where(even == 1, *chosen)


def one_hot(index, width):
    lanes = lax.broadcasted_iota(jnp.int32, (index.shape[0], width), 1)
    return (lanes == index).astype(jnp.float32).astype(jnp.bfloat16)


def mm(a, b):
    return jnp.dot(a, b, preferred_element_type=jnp.float32)


def layer_norm(values, norm_gain, offset):
    average = jnp.mean(values, axis=-1, keepdims=True)
    centred = values - average
    spread = jnp.mean(centred * centred, axis=-1, keepdims=True)
    return centred * lax.rsqrt(spread + norm_eps) * norm_gain + offset


def staged(tasks, stages):
    held = {}
    for step in range(len(tasks) + len(stages) - 1):
        for depth, stage in enumerate(stages):
            at = step - depth
            if 0 <= at < len(tasks):
                held[at] = stage(tasks[at], held.get(at))


def project(own, both, packed_ref, scale_ref, query, key, value):
    width = packed_ref.shape[1] // 3
    block = 2 * LANES
    rows = lax.broadcasted_iota(jnp.int32, (block, block), 0) // (LANES // 2)
    cols = lax.broadcasted_iota(jnp.int32, (block, block), 1) // (LANES // 2)
    same = (rows == cols).astype(jnp.float32).astype(jnp.bfloat16)
    lane = lax.broadcasted_iota(jnp.int32, (1, block), 1)
    first = (lane % LANES < LANES // 2).astype(jnp.float32)
    head = lane // (LANES // 2)
    half = both.shape[0] // 2
    tasks = []
    for j in range(width // block):
        tasks += [("q", 0, j), ("k", 0, j), ("k", 1, j), ("v", 0, j), ("v", 1, j)]

    def multiply(task, _):
        kind, part, j = task
        start = "qkv".index(kind) * width + j * block
        source = own[...] if kind == "q" else both[part * half : (part + 1) * half]
        return mm(source, packed_ref[:, start : start + block])

    def measure(task, rows):
        if task[0] == "v":
            return rows
        return rows, mm((rows * rows).astype(jnp.bfloat16), same)

    def keep(task, held):
        kind, part, j = task
        at = slice(j * block, (j + 1) * block)
        if kind == "v":
            value[part * half : (part + 1) * half, at] = held.astype(jnp.bfloat16)
            return
        rows, total = held
        rows = rows * lax.rsqrt(total + unit_eps)
        if kind == "k":
            key[part * half : (part + 1) * half, at] = rows.astype(jnp.bfloat16)
            return
        scale = jnp.zeros((1, block), jnp.float32)
        for h in range(2 * block // LANES):
            scale = jnp.where(head == h, scale_ref[j * 2 * block // LANES + h], scale)
        scale = scale * math.log2(math.e)
        left, right = rows * (scale * first), rows * (scale * (1.0 - first))
        for g in range(rows.shape[0] // GROUP):
            mine = slice(g * GROUP, (g + 1) * GROUP)
            query[2 * g * GROUP : 2 * (g + 1) * GROUP, at] = jnp.concatenate(
                [left[mine], right[mine]], axis=0
            ).astype(jnp.bfloat16)

    staged(tasks, [multiply, measure, keep])


def attend(wraps, query, key, value, open_ref, prob, ctx):
    width = query.shape[1]
    windows = len(wraps)
    pairs = query.shape[0] // windows // (2 * GROUP)
    is_first = lax.broadcasted_iota(jnp.int32, (GROUP, LANES), 1) < LANES // 2
    ones = jnp.ones((2 * GROUP, LANES), jnp.bfloat16)
    tasks = [
        (w, j, pair) for w in range(windows) for j in range(width // LANES) for pair in range(pairs)
    ]
    done = []

    def place(task):
        w, j, pair = task
        rows = slice((w * pairs + pair) * 2 * GROUP, (w * pairs + pair + 1) * 2 * GROUP)
        return rows, slice(j * LANES, (j + 1) * LANES), tasks.index(task) % prob.shape[0]

    def score(task, _):
        rows, at, slot = place(task)
        wrap, pair = wraps[task[0]], task[2]
        raw = lax.dot_general(
            query[rows, at],
            key[rows, at],
            (((1,), (1,)), ((), ())),
            preferred_element_type=jnp.float32,
        )
        raw = jnp.exp2(raw).astype(jnp.bfloat16)
        if wrap is not None or pair == pairs - 1:
            raw = raw * open_ref[pair, 0 if wrap is None else wrap]
        prob[slot] = raw

    def wait(task, _):
        return None

    def mix(task, _):
        rows, at, slot = place(task)
        out = mm(prob[slot], jnp.concatenate([value[rows, at], ones], axis=1))
        top = jnp.where(is_first, out[:GROUP, :LANES], out[GROUP:, :LANES])
        total = jnp.where(is_first, out[:GROUP, LANES:], out[GROUP:, LANES:])
        done.append(top / total)
        if len(done) == pairs:
            base = task[0] * pairs * GROUP
            ctx[base : base + pairs * GROUP, at] = jnp.concatenate(done, axis=0).astype(jnp.bfloat16)
            done.clear()

    staged(tasks, [score, wait, mix])


def attention_scratch(rows, width, depth):
    bf16 = jnp.bfloat16
    return [
        pltpu.VMEM((rows, depth), bf16),
        pltpu.VMEM((2 * rows, depth), bf16),
        pltpu.VMEM((2 * rows, width), bf16),
        pltpu.VMEM((2 * rows, width), bf16),
        pltpu.VMEM((2 * rows, width), bf16),
        pltpu.VMEM((8, 2 * GROUP, 2 * GROUP), bf16),
        pltpu.VMEM((rows, width), bf16),
    ]


def keep_window(w, mine, theirs, own, both):
    span = mine.shape[0]
    own[w * span : (w + 1) * span] = mine.astype(jnp.bfloat16)
    parts = []
    for at in range(0, span, GROUP):
        parts += [mine[at : at + GROUP], theirs[at : at + GROUP]]
    both[2 * w * span : 2 * (w + 1) * span] = jnp.concatenate(parts, axis=0).astype(jnp.bfloat16)


def block_rows(own, ctx, output_ref, gain_ref, offset_ref):
    branch = layer_norm(mm(ctx[...], output_ref[...]), gain_ref[...], offset_ref[...])
    return (own[...].astype(jnp.float32) + branch).astype(jnp.bfloat16)


def merge_rows(first, patch, merge_ref, gain_ref, offset_ref):
    cells = patch.shape[0] // 4
    channels = first.shape[1]
    part = mm(patch, first[...]).astype(jnp.bfloat16)
    total = None
    for g in range(4):
        term = mm(part[g * cells : (g + 1) * cells], merge_ref[g * channels : (g + 1) * channels])
        total = term if total is None else total + term
    return layer_norm(total, gain_ref[...], offset_ref[...]).astype(jnp.bfloat16)


def split_kernel(flags, grid_hbm, near_ref, far_ref, up_ref, down_ref, grid_ref, sem):
    fetch = pltpu.make_async_copy(grid_hbm, grid_ref, sem)
    fetch.start()
    levels, _, row_count, channels = grid_ref.shape
    lines = levels * HALF_LON
    chunks, tokens, _ = near_ref.shape
    place = lax.broadcasted_iota(jnp.int32, (row_count * lines, 1), 0)
    turn = one_hot(place % lines * row_count + place // lines, lines * row_count)
    fetch.wait()
    for side, dst in ((0, near_ref), (1, far_ref)):
        right = flags[2] if side == 0 else 1 - flags[2]
        half = grid_ref[:, pl.ds(right * HALF_LON, HALF_LON)].reshape(lines * row_count, channels)
        rows = mm(turn, half)
        for e in range(chunks):
            chunk = rows[e * tokens : (e + 1) * tokens].astype(jnp.bfloat16)
            dst[e] = chunk
            if e == 0:
                up_ref[side] = chunk
            if e == chunks - 1:
                down_ref[side] = chunk


def load_kernel(*refs):
    count = len(refs) // 2
    copies = [
        pltpu.make_async_copy(src, dst, refs[-1].at[i])
        for i, (src, dst) in enumerate(zip(refs[:count], refs[count:-1]))
    ]
    for copy in copies:
        copy.start()
    for copy in copies:
        copy.wait()


def side_kernel(
    scale_ref,
    flags,
    own_ref,
    other_ref,
    top_ref,
    bottom_ref,
    other_top_ref,
    other_bottom_ref,
    packed_ref,
    output_ref,
    gain_ref,
    offset_ref,
    merge_gain_ref,
    merge_offset_ref,
    open_ref,
    table_ref,
    merge_hbm,
    *rest,
):
    if len(rest) == 11:
        side, (merged_ref, *rest) = 0, rest
    else:
        side, (near_ref, merged_ref, up_ref, *rest) = 1, rest
    merge_ref, sem, first, own, both, query, key, value, prob, ctx = rest
    merge_copy = pltpu.make_async_copy(merge_hbm, merge_ref, sem)
    merge_copy.start()
    chunks = own_ref.shape[0]
    tokens = own_ref.shape[1]
    span = open_ref.shape[0] * GROUP
    pick = [one_hot(column_of(table_ref, PICK + s, slice(0, span)), tokens) for s in range(2)]
    lines = []
    for src, top, bottom in (
        (own_ref, top_ref[side], bottom_ref[side]),
        (other_ref, other_top_ref[0], other_bottom_ref[side]),
    ):
        lines.append([top] + [src[e] for e in range(chunks)] + [bottom])
    for w in range(chunks // 2 + 1):
        mine, theirs = (
            mm(pick[0], line[2 * w]) + mm(pick[1], line[2 * w + 1]) for line in lines
        )
        keep_window(w, mine, theirs, own, both)
    project(own, both, packed_ref, scale_ref, query, key, value)
    wraps = [flags[0]] + [None] * (chunks // 2 - 1) + [flags[1]]
    attend(wraps, query, key, value, open_ref, prob, ctx)
    first[...] = block_rows(own, ctx, output_ref, gain_ref, offset_ref)
    merge_copy.wait()
    cells = 4 * merged_ref.shape[0]
    patch = one_hot(column_of(table_ref, PATCH, slice(0, cells)), first.shape[0])
    merged = merge_rows(first, patch, merge_ref, merge_gain_ref, merge_offset_ref)
    merged_ref[...] = merged
    if side:
        count = up_ref.shape[0]
        reach = padded(count // 2)
        up_ref[...] = sum(
            mm(one_hot(column_of(table_ref, EDGE + s, slice(0, count)), reach), rows[:reach])
            for s, rows in enumerate((near_ref, merged))
        ).astype(jnp.bfloat16)


def second_kernel(
    scale_ref,
    flags,
    near_ref,
    far_ref,
    rim_ref,
    other_near_ref,
    other_far_ref,
    other_rim_ref,
    packed_ref,
    output_ref,
    gain_ref,
    offset_ref,
    open_ref,
    table_ref,
    second_ref,
    send_ref,
    return_ref,
    return_near_ref,
    own,
    both,
    query,
    key,
    value,
    prob,
    ctx,
):
    span = open_ref.shape[0] * GROUP
    windows = own.shape[0] // span
    small = rim_ref.shape[0] // 2
    for w in range(windows):
        low, high = coarse_reach(w, small, near_ref.shape[0])
        reach = [(0, low, high), (1, low, high)]
        if w == windows - 1:
            reach.append((2, 0, 2 * small))
        mine = theirs = 0.0
        for s, low, high in reach:
            at = slice(w * span, (w + 1) * span)
            pick = one_hot(column_of(table_ref, COARSE + s, at), high - low)
            mine += mm(pick, (near_ref, far_ref, rim_ref)[s][low:high])
            theirs += mm(pick, (other_near_ref, other_far_ref, other_rim_ref)[s][low:high])
        keep_window(w, mine, theirs, own, both)
    project(own, both, packed_ref, scale_ref, query, key, value)
    attend([None] * (windows - 1) + [flags[1]], query, key, value, open_ref, prob, ctx)
    second = block_rows(own, ctx, output_ref, gain_ref, offset_ref)
    second_ref[...] = second
    counts = [padded(ref.shape[0]) for ref in (send_ref, return_ref, return_near_ref)]
    index = parity_column(table_ref, SEND, 1, flags[2], slice(0, sum(counts)))
    rows = mm(one_hot(index, second.shape[0]), second).astype(jnp.bfloat16)
    at = 0
    for dst in (send_ref, return_ref, return_near_ref):
        count = dst.shape[0]
        dst[...] = rows[at : at + count]
        at += padded(count)


def place(pieces, out_ref, rows_ref, sem, low):
    rows, _, columns, pair, _ = rows_ref.shape
    block = sum(mm(one_hot(index, ref.shape[0]), ref[...]) for index, ref in pieces)
    for r in range(rows):
        for c in range(columns):
            at = (r * columns + c) * pair
            rows_ref[r, 0, c] = block[at : at + pair].astype(jnp.bfloat16)
    copy = pltpu.make_async_copy(rows_ref, out_ref.at[low : low + rows], sem)
    copy.start()
    copy.wait()


def place_columns(flags, table_ref, out_ref, which, early):
    step = out_ref.shape[2] * out_ref.shape[3]
    edge = HALF_LAT * step
    rows = slice(0, edge) if early else slice(edge, step * out_ref.shape[0])
    return [parity_column(table_ref, PLACE + s, 4, flags[2], rows) for s in which]


def late_kernel(flags, second_ref, near_ref, table_ref, out_ref, rows_ref, sem):
    index = place_columns(flags, table_ref, out_ref, (0, 1), False)
    place(zip(index, (second_ref, near_ref)), out_ref, rows_ref, sem, HALF_LAT)


def early_kernel(flags, back_ref, back_near_ref, table_ref, _, out_ref, rows_ref, sem):
    index = place_columns(flags, table_ref, out_ref, (2, 3), True)
    place(zip(index, (back_ref, back_near_ref)), out_ref, rows_ref, sem, 0)


def in_hbm(value):
    return pltpu.with_memory_space_constraint(value, pltpu.HBM)


def call(
    kernel, outs, scratch, scalars, operands, fixed=(), late=(), alias=None, held=False, room=SECOND_BYTES
):
    vmem = pl.BlockSpec(memory_space=pltpu.VMEM)
    hbm = pl.BlockSpec(memory_space=pltpu.HBM)
    fixed = [in_hbm(x) for x in fixed]
    return pl.pallas_call(
        kernel,
        out_shape=outs,
        in_specs=[pl.BlockSpec(memory_space=pltpu.SMEM)] * len(scalars)
        + [vmem] * len(operands)
        + [hbm] * len(fixed)
        + [vmem] * len(late),
        out_specs=[hbm if held else vmem] * len(outs),
        scratch_shapes=scratch,
        input_output_aliases=alias or {},
        compiler_params=pltpu.CompilerParams(vmem_limit_bytes=room),
    )(*scalars, *operands, *fixed, *late)


def far_of(i, n):
    return (i + (1 if i % 2 else -1)) % n


def near_swap(value):
    return lax.ppermute(value, "lon", [(i, i ^ 1) for i in range(lax.axis_size("lon"))])


def far_swap(value):
    n = lax.axis_size("lon")
    return lax.ppermute(value, "lon", [(i, far_of(i, n)) for i in range(n)])


def ring(value, by, turn):
    n, m = lax.axis_size("lat"), lax.axis_size("lon")
    links = [(i * m + j, (i + by) % n * m + turn(j, m)) for i in range(n) for j in range(m)]
    return lax.ppermute(value, ("lat", "lon"), links)


def shift(value, by):
    n = lax.axis_size("lat")
    return lax.ppermute(value, "lat", [(i, i + by) for i in range(n) if 0 <= i + by < n])


def body(
    features,
    packed_first,
    scale_first,
    output_first,
    gain_first,
    offset_first,
    merge_weight,
    merge_gain,
    merge_offset,
    packed_second,
    scale_second,
    output_second,
    gain_second,
    offset_second,
):
    levels, row_count, col_count, channels = features.shape
    inner = packed_first.shape[1] // 3
    second_inner = packed_second.shape[1] // 3
    wide = merge_weight.shape[1]
    half_rows = row_count // 2
    lat_pos = lax.axis_index("lat")
    odd = lax.axis_index("lon") % 2
    last = lax.axis_size("lat") - 1
    place = jnp.stack([lat_pos, lat_pos, 1 - odd])
    flags = (place == jnp.asarray([0, last, 1], jnp.int32)).astype(jnp.int32)
    bf16 = jnp.bfloat16
    span = levels // WLEV * GROUP
    tokens = HALF_LAT * levels * HALF_LON
    chunks = row_count // HALF_LAT
    windows = chunks // 2 + 1

    half = jax.ShapeDtypeStruct((chunks, tokens, channels), bf16)
    ends = jax.ShapeDtypeStruct((2, tokens, channels), bf16)
    near, far, ups, downs = call(
        split_kernel,
        [half, half, ends, ends],
        [pltpu.VMEM((levels, col_count, row_count, channels), bf16), pltpu.SemaphoreType.DMA],
        [flags],
        [],
        [jnp.transpose(features, (0, 2, 1, 3))],
    )
    bottom = shift(ups, -1)
    top = shift(downs, 1)
    near_other = near_swap(near)
    far_other = far_swap(far)
    near_other_top, near_other_bottom = near_swap(top), near_swap(bottom)
    far_rim = far_swap(jnp.stack([top[1], bottom[1]]))

    opened = jnp.asarray(open_tables(levels), bf16)
    cells = half_rows * levels * HALF_LON // 2
    small = jax.ShapeDtypeStruct((cells, wide), bf16)
    edge = jax.ShapeDtypeStruct((tokens, wide), bf16)

    shared = [packed_first, output_first, gain_first[None], offset_first[None]]
    shared += [merge_gain[None], merge_offset[None], opened]
    shared += [jnp.asarray(index_table(levels, row_count))]
    shared = call(
        load_kernel,
        [jax.ShapeDtypeStruct(x.shape, x.dtype) for x in shared],
        [pltpu.SemaphoreType.DMA((len(shared),))],
        [],
        [],
        shared,
    )
    shared = list(shared)
    opened, table = shared[-2:]
    buffers = [pltpu.VMEM(merge_weight.shape, bf16), pltpu.SemaphoreType.DMA]
    buffers += [pltpu.VMEM((windows * span, channels), bf16)]
    buffers += attention_scratch(windows * span, inner, channels)
    (merged_near,) = call(
        side_kernel,
        [small],
        buffers,
        [in_hbm(scale_first), flags],
        [near, near_other, top, bottom, near_other_top, near_other_bottom] + shared,
        [merge_weight],
        room=FIRST_BYTES,
    )
    other_near = far_swap(merged_near)
    merged_far, edge_up = call(
        side_kernel,
        [small, edge],
        buffers,
        [in_hbm(scale_first), flags],
        [far, far_other, top, bottom, far_rim, far_rim] + shared,
        [merge_weight],
        [merged_near],
        room=FIRST_BYTES,
    )
    other_far = far_swap(merged_far)
    other_rim = ring(edge_up, -1, far_of)
    rim = ring(edge_up, -1, lambda j, m: j)

    windows = half_rows // WLAT
    share = levels // 2 * HALF_LON

    back = jax.ShapeDtypeStruct((HALF_LAT * share, wide), bf16)
    second, send, back_same, back_near = call(
        second_kernel,
        [
            jax.ShapeDtypeStruct((windows * span, wide), bf16),
            jax.ShapeDtypeStruct(((half_rows - HALF_LAT) * share, wide), bf16),
            back,
            back,
        ],
        attention_scratch(windows * span, second_inner, wide),
        [in_hbm(scale_second), flags],
        [
            merged_near,
            merged_far,
            rim,
            other_near,
            other_far,
            other_rim,
            packed_second,
            output_second,
            gain_second[None],
            offset_second[None],
            opened,
            table,
        ],
    )
    back_near = ring(back_near, 1, lambda j, m: j ^ 1)
    back_same = ring(back_same, 1, lambda j, m: j)
    received = near_swap(send)
    shape = (half_rows, 1, WLON, levels // 2, wide)
    whole = [jax.ShapeDtypeStruct(shape, bf16)]

    def room(rows):
        return [pltpu.VMEM((rows,) + shape[1:], bf16), pltpu.SemaphoreType.DMA]

    (out,) = call(
        late_kernel,
        whole,
        room(half_rows - HALF_LAT),
        [flags],
        [second, received, table],
        held=True,
    )
    (out,) = call(
        early_kernel,
        whole,
        room(HALF_LAT),
        [flags],
        [back_same, back_near, table],
        [out],
        alias={4: 0},
        held=True,
    )
    return jnp.transpose(out, (0, 1, 3, 2, 4))


def solution(mesh):
    return jax.shard_map(
        body,
        mesh=mesh,
        in_specs=(P(None, "lat", "lon", None),) + (P(),) * 13,
        out_specs=P("lat", "lon", None, None, None),
        check_vma=False,
    )
```

```python
import math

import jax
import jax.numpy as jnp
import numpy as np
from jax import lax
from jax.experimental import pallas as pl
from jax.experimental.pallas import tpu as pltpu
from jax.sharding import PartitionSpec as P

WLEV = 2
WLAT = 6
WLON = 12
HALF_LAT = WLAT // 2
HALF_LON = WLON // 2
LANES = 128
FIRST_BYTES, SECOND_BYTES = 48 << 20, 32 << 20

norm_eps = 1e-05
unit_eps = 1e-06

PART = WLEV * HALF_LAT * HALF_LON
GROUP = 2 * PART


def rolled_levels(levels):
    return [(l + WLEV // 2) % levels for l in range(levels)]


def window_slots(levels):
    order = rolled_levels(levels)
    for place, level in enumerate(order):
        pair, lev = divmod(place, WLEV)
        for side in range(2):
            for i in range(HALF_LAT):
                for c in range(HALF_LON):
                    t = (i * WLEV + lev) * HALF_LON + c
                    yield pair * GROUP + side * PART + t, side, level, i, c


def slot_table(levels):
    table = {}
    for row, side, level, i, c in window_slots(levels):
        table[(side, level, i, c)] = row
    return table


def column(values):
    return np.asarray(values, np.int32).reshape(-1, 1)


def fine_gather(levels):
    rows = levels // WLEV * GROUP
    out = [np.full(rows, -1), np.full(rows, -1)]
    for row, side, level, i, c in window_slots(levels):
        out[side][row] = (i * levels + level) * HALF_LON + c
    return column(out[0]), column(out[1])


def patch_gather(levels, row_count):
    span = levels // WLEV * GROUP
    slots = slot_table(levels)
    out = []
    for g in range(4):
        dc, dr = divmod(g, 2)
        rows = []
        for i in range(row_count // 2):
            for level in range(levels):
                for cc in range(HALF_LON // 2):
                    r = 2 * i + dr
                    chunk = r // HALF_LAT + 1
                    w, side = divmod(chunk, 2)
                    rows.append(w * span + slots[(side, level, r % HALF_LAT, 2 * cc + dc)])
        out.append(column(rows))
    return np.concatenate(out)


def coarse_gather(levels, row_count):
    span = levels // WLEV * GROUP
    chunks = row_count // HALF_LAT
    third = HALF_LON // 2
    small = HALF_LAT * levels * third
    out = np.full((3, chunks // 2 * span, 1), -(1 << 20), np.int32)
    for w in range(chunks // 2):
        for row, side, level, i, c in window_slots(levels):
            chunk = 2 * w + side + 1
            which, cc = divmod(c, third)
            cell = (i * levels + level) * third + cc
            at = w * span + row
            if chunk < chunks:
                low = coarse_reach(w, small, chunks * small)[0]
                out[which, at, 0] = chunk * small + cell - low
            else:
                out[2, at, 0] = which * small + cell
    return out


def coarse_reach(w, small, count):
    return (2 * w + 1) * small // 16 * 16, min(padded((2 * w + 3) * small), count)


def edge_gather(levels):
    small = HALF_LAT * levels * HALF_LON // 2
    out = np.full((2, 2 * small, 1), -1, np.int32)
    for which in range(2):
        out[which, which * small : (which + 1) * small, 0] = np.arange(small)
    return out


def coarse_slot(levels, even, r, level, c):
    third = HALF_LON // 2
    place = (c + third) % HALF_LON if even else c
    w, side = divmod(r // HALF_LAT - 1, 2)
    return w * (levels // WLEV * GROUP) + slot_table(levels)[(side, level, r % HALF_LAT, place)]


def padded(count):
    return -(-count // 16) * 16


def send_gather(levels, row_count, even):
    half = levels // 2
    mine, theirs = (0, half) if even else (half, 0)
    parts = []
    for base, low, high in (
        (theirs, HALF_LAT, row_count),
        (mine, row_count, row_count + HALF_LAT),
        (theirs, row_count, row_count + HALF_LAT),
    ):
        rows = [
            coarse_slot(levels, even, r, base + e, c)
            for r in range(low, high)
            for e in range(half)
            for c in range(HALF_LON)
        ]
        parts += rows + [-1] * (padded(len(rows)) - len(rows))
    return column(parts)


def place_gather(levels, row_count, even):
    half = levels // 2
    out = np.full((4, row_count, WLON, half), -1)
    base = 0 if even else half
    for r in range(row_count):
        for e in range(half):
            for c in range(HALF_LON):
                mine, theirs = (c, c + HALF_LON) if even else (c + HALF_LON, c)
                if r >= HALF_LAT:
                    out[0, r, mine, e] = coarse_slot(levels, even, r, base + e, c)
                    out[1, r, theirs, e] = ((r - HALF_LAT) * half + e) * HALF_LON + c
                else:
                    out[2, r, mine, e] = (r * half + e) * HALF_LON + c
                    out[3, r, theirs, e] = (r * half + e) * HALF_LON + c
    return out.reshape(4, -1, 1).astype(np.int32)


def open_tables(levels):
    order = rolled_levels(levels)
    sides = np.arange(GROUP) // PART
    levs = np.arange(GROUP) % PART // HALF_LON % WLEV
    out = np.zeros((levels // WLEV, 2, GROUP, GROUP), np.float32)
    for pair in range(levels // WLEV):
        wrapped = np.asarray([order[pair * WLEV + v] < WLEV // 2 for v in range(WLEV)])[levs]
        seen = wrapped[:, None] == wrapped[None]
        out[pair, 0] = seen
        out[pair, 1] = seen & (sides[:, None] == sides[None])
    return np.tile(out, (1, 1, 2, 2))


PATCH, PICK, EDGE, COARSE, SEND, PLACE = 0, 1, 3, 5, 8, 10


def index_table(levels, row_count):
    half_rows = row_count // 2
    columns = [patch_gather(levels, row_count), *fine_gather(levels), *edge_gather(levels)]
    columns += [*coarse_gather(levels, half_rows)]
    columns += [send_gather(levels, half_rows, even) for even in (False, True)]
    for even in (False, True):
        columns += [*place_gather(levels, half_rows, even)]
    out = np.full((padded(max(len(c) for c in columns)), len(columns)), -(1 << 20), np.int32)
    for at, values in enumerate(columns):
        out[: len(values), at] = values[:, 0]
    return out


def column_of(table_ref, at, rows):
    return table_ref[rows, at : at + 1]


def parity_column(table_ref, at, step, even, rows):
    chosen = column_of(table_ref, at + step, rows), column_of(table_ref, at, rows)
    return jnp.where(even == 1, *chosen)


def one_hot(index, width):
    lanes = lax.broadcasted_iota(jnp.int32, (index.shape[0], width), 1)
    return (lanes == index).astype(jnp.float32).astype(jnp.bfloat16)


def mm(a, b):
    return jnp.dot(a, b, preferred_element_type=jnp.float32)


def layer_norm(values, norm_gain, offset):
    average = jnp.mean(values, axis=-1, keepdims=True)
    centred = values - average
    spread = jnp.mean(centred * centred, axis=-1, keepdims=True)
    return centred * lax.rsqrt(spread + norm_eps) * norm_gain + offset


def staged(tasks, stages):
    held = {}
    for step in range(len(tasks) + len(stages) - 1):
        for depth, stage in enumerate(stages):
            at = step - depth
            if 0 <= at < len(tasks):
                held[at] = stage(tasks[at], held.get(at))


def project(own, both, packed_ref, scale_ref, query, key, value):
    width = packed_ref.shape[1] // 3
    block = 2 * LANES
    rows = lax.broadcasted_iota(jnp.int32, (block, block), 0) // (LANES // 2)
    cols = lax.broadcasted_iota(jnp.int32, (block, block), 1) // (LANES // 2)
    same = (rows == cols).astype(jnp.float32).astype(jnp.bfloat16)
    lane = lax.broadcasted_iota(jnp.int32, (1, block), 1)
    first = (lane % LANES < LANES // 2).astype(jnp.float32)
    head = lane // (LANES // 2)
    half = both.shape[0] // 2
    tasks = []
    for j in range(width // block):
        tasks += [("q", 0, j), ("k", 0, j), ("k", 1, j), ("v", 0, j), ("v", 1, j)]

    def multiply(task, _):
        kind, part, j = task
        start = "qkv".index(kind) * width + j * block
        source = own[...] if kind == "q" else both[part * half : (part + 1) * half]
        return mm(source, packed_ref[:, start : start + block])

    def measure(task, rows):
        if task[0] == "v":
            return rows
        return rows, mm((rows * rows).astype(jnp.bfloat16), same)

    def keep(task, held):
        kind, part, j = task
        at = slice(j * block, (j + 1) * block)
        if kind == "v":
            value[part * half : (part + 1) * half, at] = held.astype(jnp.bfloat16)
            return
        rows, total = held
        rows = rows * lax.rsqrt(total + unit_eps)
        if kind == "k":
            key[part * half : (part + 1) * half, at] = rows.astype(jnp.bfloat16)
            return
        scale = jnp.zeros((1, block), jnp.float32)
        for h in range(2 * block // LANES):
            scale = jnp.where(head == h, scale_ref[j * 2 * block // LANES + h], scale)
        scale = scale * math.log2(math.e)
        left, right = rows * (scale * first), rows * (scale * (1.0 - first))
        for g in range(rows.shape[0] // GROUP):
            mine = slice(g * GROUP, (g + 1) * GROUP)
            query[2 * g * GROUP : 2 * (g + 1) * GROUP, at] = jnp.concatenate(
                [left[mine], right[mine]], axis=0
            ).astype(jnp.bfloat16)

    staged(tasks, [multiply, measure, keep])


def attend(wraps, query, key, value, open_ref, prob, ctx):
    width = query.shape[1]
    windows = len(wraps)
    pairs = query.shape[0] // windows // (2 * GROUP)
    is_first = lax.broadcasted_iota(jnp.int32, (GROUP, LANES), 1) < LANES // 2
    ones = jnp.ones((2 * GROUP, LANES), jnp.bfloat16)
    tasks = [
        (w, j, pair) for w in range(windows) for j in range(width // LANES) for pair in range(pairs)
    ]
    done = []

    def place(task):
        w, j, pair = task
        rows = slice((w * pairs + pair) * 2 * GROUP, (w * pairs + pair + 1) * 2 * GROUP)
        return rows, slice(j * LANES, (j + 1) * LANES), tasks.index(task) % prob.shape[0]

    def score(task, _):
        rows, at, slot = place(task)
        wrap, pair = wraps[task[0]], task[2]
        raw = lax.dot_general(
            query[rows, at],
            key[rows, at],
            (((1,), (1,)), ((), ())),
            preferred_element_type=jnp.float32,
        )
        raw = jnp.exp2(raw).astype(jnp.bfloat16)
        if wrap is not None or pair == pairs - 1:
            raw = raw * open_ref[pair, 0 if wrap is None else wrap]
        prob[slot] = raw

    def wait(task, _):
        return None

    def mix(task, _):
        rows, at, slot = place(task)
        out = mm(prob[slot], jnp.concatenate([value[rows, at], ones], axis=1))
        top = jnp.where(is_first, out[:GROUP, :LANES], out[GROUP:, :LANES])
        total = jnp.where(is_first, out[:GROUP, LANES:], out[GROUP:, LANES:])
        done.append(top / total)
        if len(done) == pairs:
            base = task[0] * pairs * GROUP
            ctx[base : base + pairs * GROUP, at] = jnp.concatenate(done, axis=0).astype(jnp.bfloat16)
            done.clear()

    staged(tasks, [score, wait, mix])


def attention_scratch(rows, width, depth):
    bf16 = jnp.bfloat16
    return [
        pltpu.VMEM((rows, depth), bf16),
        pltpu.VMEM((2 * rows, depth), bf16),
        pltpu.VMEM((2 * rows, width), bf16),
        pltpu.VMEM((2 * rows, width), bf16),
        pltpu.VMEM((2 * rows, width), bf16),
        pltpu.VMEM((8, 2 * GROUP, 2 * GROUP), bf16),
        pltpu.VMEM((rows, width), bf16),
    ]


def keep_window(w, mine, theirs, own, both):
    span = mine.shape[0]
    own[w * span : (w + 1) * span] = mine.astype(jnp.bfloat16)
    parts = []
    for at in range(0, span, GROUP):
        parts += [mine[at : at + GROUP], theirs[at : at + GROUP]]
    both[2 * w * span : 2 * (w + 1) * span] = jnp.concatenate(parts, axis=0).astype(jnp.bfloat16)


def block_rows(own, ctx, output_ref, gain_ref, offset_ref):
    branch = layer_norm(mm(ctx[...], output_ref[...]), gain_ref[...], offset_ref[...])
    return (own[...].astype(jnp.float32) + branch).astype(jnp.bfloat16)


def merge_rows(first, patch, merge_ref, gain_ref, offset_ref):
    cells = patch.shape[0] // 4
    channels = first.shape[1]
    part = mm(patch, first[...]).astype(jnp.bfloat16)
    total = None
    for g in range(4):
        term = mm(part[g * cells : (g + 1) * cells], merge_ref[g * channels : (g + 1) * channels])
        total = term if total is None else total + term
    return layer_norm(total, gain_ref[...], offset_ref[...]).astype(jnp.bfloat16)


def split_kernel(flags, grid_hbm, near_ref, far_ref, up_ref, down_ref, grid_ref, sem):
    fetch = pltpu.make_async_copy(grid_hbm, grid_ref, sem)
    fetch.start()
    levels, _, row_count, channels = grid_ref.shape
    lines = levels * HALF_LON
    chunks, tokens, _ = near_ref.shape
    place = lax.broadcasted_iota(jnp.int32, (row_count * lines, 1), 0)
    turn = one_hot(place % lines * row_count + place // lines, lines * row_count)
    fetch.wait()
    for side, dst in ((0, near_ref), (1, far_ref)):
        right = flags[2] if side == 0 else 1 - flags[2]
        half = grid_ref[:, pl.ds(right * HALF_LON, HALF_LON)].reshape(lines * row_count, channels)
        rows = mm(turn, half)
        for e in range(chunks):
            chunk = rows[e * tokens : (e + 1) * tokens].astype(jnp.bfloat16)
            dst[e] = chunk
            if e == 0:
                up_ref[side] = chunk
            if e == chunks - 1:
                down_ref[side] = chunk


def load_kernel(*refs):
    count = len(refs) // 2
    copies = [
        pltpu.make_async_copy(src, dst, refs[-1].at[i])
        for i, (src, dst) in enumerate(zip(refs[:count], refs[count:-1]))
    ]
    for copy in copies:
        copy.start()
    for copy in copies:
        copy.wait()


def first_windows(
    lines, wraps, table_ref, packed_ref, scale_ref, output_ref, gain_ref, offset_ref, open_ref, scratch
):
    own, both, query, key, value, prob, ctx = scratch
    tokens = lines[0][0].shape[0]
    span = open_ref.shape[0] * GROUP
    pick = [one_hot(column_of(table_ref, PICK + s, slice(0, span)), tokens) for s in range(2)]
    for w in range(len(wraps)):
        mine, theirs = (
            mm(pick[0], line[2 * w]) + mm(pick[1], line[2 * w + 1]) for line in lines
        )
        keep_window(w, mine, theirs, own, both)
    project(own, both, packed_ref, scale_ref, query, key, value)
    attend(wraps, query, key, value, open_ref, prob, ctx)
    return block_rows(own, ctx, output_ref, gain_ref, offset_ref)


def inner_kernel(
    scale_ref,
    own_ref,
    other_ref,
    packed_ref,
    output_ref,
    gain_ref,
    offset_ref,
    open_ref,
    table_ref,
    rows_ref,
    *scratch,
):
    chunks = own_ref.shape[0]
    lines = [[ref[e] for e in range(1, chunks - 1)] for ref in (own_ref, other_ref)]
    rows_ref[...] = first_windows(
        lines,
        [None] * (chunks // 2 - 1),
        table_ref,
        packed_ref,
        scale_ref,
        output_ref,
        gain_ref,
        offset_ref,
        open_ref,
        scratch,
    )


def side_kernel(
    scale_ref,
    flags,
    own_ref,
    other_ref,
    top_ref,
    bottom_ref,
    other_top_ref,
    other_bottom_ref,
    packed_ref,
    output_ref,
    gain_ref,
    offset_ref,
    merge_gain_ref,
    merge_offset_ref,
    open_ref,
    table_ref,
    merge_hbm,
    *rest,
):
    if len(rest) == 12:
        side, (inner_ref, merged_ref, *rest) = 0, rest
    else:
        side, (near_ref, merged_ref, up_ref, *rest) = 1, rest
    merge_ref, sem, first, *scratch = rest
    merge_copy = pltpu.make_async_copy(merge_hbm, merge_ref, sem)
    merge_copy.start()
    chunks = own_ref.shape[0]
    span = open_ref.shape[0] * GROUP
    inside = range(chunks) if side else (0, chunks - 1)
    lines = []
    for src, top, bottom in (
        (own_ref, top_ref[side], bottom_ref[side]),
        (other_ref, other_top_ref[0], other_bottom_ref[side]),
    ):
        lines.append([top] + [src[e] for e in inside] + [bottom])
    wraps = [flags[0]] + [None] * (len(inside) // 2 - 1) + [flags[1]]
    rows = first_windows(
        lines,
        wraps,
        table_ref,
        packed_ref,
        scale_ref,
        output_ref,
        gain_ref,
        offset_ref,
        open_ref,
        scratch,
    )
    if side:
        first[...] = rows
    else:
        first[:span] = rows[:span]
        first[span : first.shape[0] - span] = inner_ref[...]
        first[first.shape[0] - span :] = rows[span:]
    merge_copy.wait()
    cells = 4 * merged_ref.shape[0]
    patch = one_hot(column_of(table_ref, PATCH, slice(0, cells)), first.shape[0])
    merged = merge_rows(first, patch, merge_ref, merge_gain_ref, merge_offset_ref)
    merged_ref[...] = merged
    if side:
        count = up_ref.shape[0]
        reach = padded(count // 2)
        up_ref[...] = sum(
            mm(one_hot(column_of(table_ref, EDGE + s, slice(0, count)), reach), rows[:reach])
            for s, rows in enumerate((near_ref, merged))
        ).astype(jnp.bfloat16)


def second_kernel(
    scale_ref,
    flags,
    near_ref,
    far_ref,
    rim_ref,
    other_near_ref,
    other_far_ref,
    other_rim_ref,
    packed_ref,
    output_ref,
    gain_ref,
    offset_ref,
    open_ref,
    table_ref,
    second_ref,
    send_ref,
    return_ref,
    return_near_ref,
    own,
    both,
    query,
    key,
    value,
    prob,
    ctx,
):
    span = open_ref.shape[0] * GROUP
    windows = own.shape[0] // span
    small = rim_ref.shape[0] // 2
    for w in range(windows):
        low, high = coarse_reach(w, small, near_ref.shape[0])
        reach = [(0, low, high), (1, low, high)]
        if w == windows - 1:
            reach.append((2, 0, 2 * small))
        mine = theirs = 0.0
        for s, low, high in reach:
            at = slice(w * span, (w + 1) * span)
            pick = one_hot(column_of(table_ref, COARSE + s, at), high - low)
            mine += mm(pick, (near_ref, far_ref, rim_ref)[s][low:high])
            theirs += mm(pick, (other_near_ref, other_far_ref, other_rim_ref)[s][low:high])
        keep_window(w, mine, theirs, own, both)
    project(own, both, packed_ref, scale_ref, query, key, value)
    attend([None] * (windows - 1) + [flags[1]], query, key, value, open_ref, prob, ctx)
    second = block_rows(own, ctx, output_ref, gain_ref, offset_ref)
    second_ref[...] = second
    counts = [padded(ref.shape[0]) for ref in (send_ref, return_ref, return_near_ref)]
    index = parity_column(table_ref, SEND, 1, flags[2], slice(0, sum(counts)))
    rows = mm(one_hot(index, second.shape[0]), second).astype(jnp.bfloat16)
    at = 0
    for dst in (send_ref, return_ref, return_near_ref):
        count = dst.shape[0]
        dst[...] = rows[at : at + count]
        at += padded(count)


def place(pieces, out_ref, rows_ref, sem, low):
    rows, _, columns, pair, _ = rows_ref.shape
    block = sum(mm(one_hot(index, ref.shape[0]), ref[...]) for index, ref in pieces)
    for r in range(rows):
        for c in range(columns):
            at = (r * columns + c) * pair
            rows_ref[r, 0, c] = block[at : at + pair].astype(jnp.bfloat16)
    copy = pltpu.make_async_copy(rows_ref, out_ref.at[low : low + rows], sem)
    copy.start()
    copy.wait()


def place_columns(flags, table_ref, out_ref, which, early):
    step = out_ref.shape[2] * out_ref.shape[3]
    edge = HALF_LAT * step
    rows = slice(0, edge) if early else slice(edge, step * out_ref.shape[0])
    return [parity_column(table_ref, PLACE + s, 4, flags[2], rows) for s in which]


def late_kernel(flags, second_ref, near_ref, table_ref, out_ref, rows_ref, sem):
    index = place_columns(flags, table_ref, out_ref, (0, 1), False)
    place(zip(index, (second_ref, near_ref)), out_ref, rows_ref, sem, HALF_LAT)


def early_kernel(flags, back_ref, back_near_ref, table_ref, _, out_ref, rows_ref, sem):
    index = place_columns(flags, table_ref, out_ref, (2, 3), True)
    place(zip(index, (back_ref, back_near_ref)), out_ref, rows_ref, sem, 0)


def in_hbm(value):
    return pltpu.with_memory_space_constraint(value, pltpu.HBM)


def call(
    kernel, outs, scratch, scalars, operands, fixed=(), late=(), alias=None, held=False, room=SECOND_BYTES
):
    vmem = pl.BlockSpec(memory_space=pltpu.VMEM)
    hbm = pl.BlockSpec(memory_space=pltpu.HBM)
    fixed = [in_hbm(x) for x in fixed]
    return pl.pallas_call(
        kernel,
        out_shape=outs,
        in_specs=[pl.BlockSpec(memory_space=pltpu.SMEM)] * len(scalars)
        + [vmem] * len(operands)
        + [hbm] * len(fixed)
        + [vmem] * len(late),
        out_specs=[hbm if held else vmem] * len(outs),
        scratch_shapes=scratch,
        input_output_aliases=alias or {},
        compiler_params=pltpu.CompilerParams(vmem_limit_bytes=room),
    )(*scalars, *operands, *fixed, *late)


def far_of(i, n):
    return (i + (1 if i % 2 else -1)) % n


def near_swap(value):
    return lax.ppermute(value, "lon", [(i, i ^ 1) for i in range(lax.axis_size("lon"))])


def far_swap(value):
    n = lax.axis_size("lon")
    return lax.ppermute(value, "lon", [(i, far_of(i, n)) for i in range(n)])


def ring(value, by, turn):
    n, m = lax.axis_size("lat"), lax.axis_size("lon")
    links = [(i * m + j, (i + by) % n * m + turn(j, m)) for i in range(n) for j in range(m)]
    return lax.ppermute(value, ("lat", "lon"), links)


def shift(value, by):
    n = lax.axis_size("lat")
    return lax.ppermute(value, "lat", [(i, i + by) for i in range(n) if 0 <= i + by < n])


def body(
    features,
    packed_first,
    scale_first,
    output_first,
    gain_first,
    offset_first,
    merge_weight,
    merge_gain,
    merge_offset,
    packed_second,
    scale_second,
    output_second,
    gain_second,
    offset_second,
):
    levels, row_count, col_count, channels = features.shape
    inner = packed_first.shape[1] // 3
    second_inner = packed_second.shape[1] // 3
    wide = merge_weight.shape[1]
    half_rows = row_count // 2
    lat_pos = lax.axis_index("lat")
    odd = lax.axis_index("lon") % 2
    last = lax.axis_size("lat") - 1
    place = jnp.stack([lat_pos, lat_pos, 1 - odd])
    flags = (place == jnp.asarray([0, last, 1], jnp.int32)).astype(jnp.int32)
    bf16 = jnp.bfloat16
    span = levels // WLEV * GROUP
    tokens = HALF_LAT * levels * HALF_LON
    chunks = row_count // HALF_LAT
    windows = chunks // 2 + 1

    half = jax.ShapeDtypeStruct((chunks, tokens, channels), bf16)
    ends = jax.ShapeDtypeStruct((2, tokens, channels), bf16)
    near, far, ups, downs = call(
        split_kernel,
        [half, half, ends, ends],
        [pltpu.VMEM((levels, col_count, row_count, channels), bf16), pltpu.SemaphoreType.DMA],
        [flags],
        [],
        [jnp.transpose(features, (0, 2, 1, 3))],
    )
    bottom = shift(ups, -1)
    top = shift(downs, 1)
    near_other = near_swap(near)
    far_other = far_swap(far)
    near_other_top, near_other_bottom = near_swap(top), near_swap(bottom)
    far_rim = far_swap(jnp.stack([top[1], bottom[1]]))

    opened = jnp.asarray(open_tables(levels), bf16)
    cells = half_rows * levels * HALF_LON // 2
    small = jax.ShapeDtypeStruct((cells, wide), bf16)
    edge = jax.ShapeDtypeStruct((tokens, wide), bf16)

    shared = [packed_first, output_first, gain_first[None], offset_first[None]]
    shared += [merge_gain[None], merge_offset[None], opened]
    shared += [jnp.asarray(index_table(levels, row_count))]
    shared = call(
        load_kernel,
        [jax.ShapeDtypeStruct(x.shape, x.dtype) for x in shared],
        [pltpu.SemaphoreType.DMA((len(shared),))],
        [],
        [],
        shared,
    )
    shared = list(shared)
    opened, table = shared[-2:]
    buffers = [pltpu.VMEM(merge_weight.shape, bf16), pltpu.SemaphoreType.DMA]
    buffers += [pltpu.VMEM((windows * span, channels), bf16)]
    (inner_rows,) = call(
        inner_kernel,
        [jax.ShapeDtypeStruct(((windows - 2) * span, channels), bf16)],
        attention_scratch((windows - 2) * span, inner, channels),
        [in_hbm(scale_first)],
        [near, near_other] + shared[:4] + shared[-2:],
    )
    (merged_near,) = call(
        side_kernel,
        [small],
        buffers + attention_scratch(2 * span, inner, channels),
        [in_hbm(scale_first), flags],
        [near, near_other, top, bottom, near_other_top, near_other_bottom] + shared,
        [merge_weight],
        [inner_rows],
        room=FIRST_BYTES,
    )
    other_near = far_swap(merged_near)
    merged_far, edge_up = call(
        side_kernel,
        [small, edge],
        buffers + attention_scratch(windows * span, inner, channels),
        [in_hbm(scale_first), flags],
        [far, far_other, top, bottom, far_rim, far_rim] + shared,
        [merge_weight],
        [merged_near],
        room=FIRST_BYTES,
    )
    other_far = far_swap(merged_far)
    other_rim = ring(edge_up, -1, far_of)
    rim = ring(edge_up, -1, lambda j, m: j)

    windows = half_rows // WLAT
    share = levels // 2 * HALF_LON

    back = jax.ShapeDtypeStruct((HALF_LAT * share, wide), bf16)
    second, send, back_same, back_near = call(
        second_kernel,
        [
            jax.ShapeDtypeStruct((windows * span, wide), bf16),
            jax.ShapeDtypeStruct(((half_rows - HALF_LAT) * share, wide), bf16),
            back,
            back,
        ],
        attention_scratch(windows * span, second_inner, wide),
        [in_hbm(scale_second), flags],
        [
            merged_near,
            merged_far,
            rim,
            other_near,
            other_far,
            other_rim,
            packed_second,
            output_second,
            gain_second[None],
            offset_second[None],
            opened,
            table,
        ],
    )
    back_near = ring(back_near, 1, lambda j, m: j ^ 1)
    back_same = ring(back_same, 1, lambda j, m: j)
    received = near_swap(send)
    shape = (half_rows, 1, WLON, levels // 2, wide)
    whole = [jax.ShapeDtypeStruct(shape, bf16)]

    def room(rows):
        return [pltpu.VMEM((rows,) + shape[1:], bf16), pltpu.SemaphoreType.DMA]

    (out,) = call(
        late_kernel,
        whole,
        room(half_rows - HALF_LAT),
        [flags],
        [second, received, table],
        held=True,
    )
    (out,) = call(
        early_kernel,
        whole,
        room(HALF_LAT),
        [flags],
        [back_same, back_near, table],
        [out],
        alias={4: 0},
        held=True,
    )
    return jnp.transpose(out, (0, 1, 3, 2, 4))


def solution(mesh):
    return jax.shard_map(
        body,
        mesh=mesh,
        in_specs=(P(None, "lat", "lon", None),) + (P(),) * 13,
        out_specs=P("lat", "lon", None, None, None),
        check_vma=False,
    )
```

```python
import functools
import math

import jax
import jax.numpy as jnp
import numpy as np
from jax import lax
from jax.experimental import pallas as pl
from jax.experimental.pallas import tpu as pltpu
from jax.sharding import PartitionSpec as P

WLEV = 2
WLAT = 6
WLON = 12
HALF_LAT = WLAT // 2
HALF_LON = WLON // 2
LANES = 128
FIRST_BYTES, SECOND_BYTES = 48 << 20, 32 << 20

norm_eps = 1e-05
unit_eps = 1e-06

PART = WLEV * HALF_LAT * HALF_LON
GROUP = 2 * PART


def rolled_levels(levels):
    return [(l + WLEV // 2) % levels for l in range(levels)]


def window_slots(levels):
    order = rolled_levels(levels)
    for place, level in enumerate(order):
        pair, lev = divmod(place, WLEV)
        for side in range(2):
            for i in range(HALF_LAT):
                for c in range(HALF_LON):
                    t = (i * WLEV + lev) * HALF_LON + c
                    yield pair * GROUP + side * PART + t, side, level, i, c


def slot_table(levels):
    table = {}
    for row, side, level, i, c in window_slots(levels):
        table[(side, level, i, c)] = row
    return table


def column(values):
    return np.asarray(values, np.int32).reshape(-1, 1)


def fine_gather(levels):
    rows = levels // WLEV * GROUP
    out = [np.full(rows, -1), np.full(rows, -1)]
    for row, side, level, i, c in window_slots(levels):
        out[side][row] = (i * levels + level) * HALF_LON + c
    return column(out[0]), column(out[1])


def patch_gather(levels, row_count):
    span = levels // WLEV * GROUP
    slots = slot_table(levels)
    out = []
    for g in range(4):
        dc, dr = divmod(g, 2)
        rows = []
        for i in range(row_count // 2):
            for level in range(levels):
                for cc in range(HALF_LON // 2):
                    r = 2 * i + dr
                    chunk = r // HALF_LAT + 1
                    w, side = divmod(chunk, 2)
                    rows.append(w * span + slots[(side, level, r % HALF_LAT, 2 * cc + dc)])
        out.append(column(rows))
    return np.concatenate(out)


def coarse_gather(levels, row_count):
    span = levels // WLEV * GROUP
    chunks = row_count // HALF_LAT
    third = HALF_LON // 2
    small = HALF_LAT * levels * third
    out = np.full((3, chunks // 2 * span, 1), -(1 << 20), np.int32)
    for w in range(chunks // 2):
        for row, side, level, i, c in window_slots(levels):
            chunk = 2 * w + side + 1
            which, cc = divmod(c, third)
            cell = (i * levels + level) * third + cc
            at = w * span + row
            if chunk < chunks:
                low = coarse_reach(w, small, chunks * small)[0]
                out[which, at, 0] = chunk * small + cell - low
            else:
                out[2, at, 0] = which * small + cell
    return out


def coarse_reach(w, small, count):
    return (2 * w + 1) * small // 16 * 16, min(padded((2 * w + 3) * small), count)


def edge_gather(levels):
    small = HALF_LAT * levels * HALF_LON // 2
    out = np.full((2, 2 * small, 1), -1, np.int32)
    for which in range(2):
        out[which, which * small : (which + 1) * small, 0] = np.arange(small)
    return out


def coarse_slot(levels, even, r, level, c):
    third = HALF_LON // 2
    place = (c + third) % HALF_LON if even else c
    w, side = divmod(r // HALF_LAT - 1, 2)
    return w * (levels // WLEV * GROUP) + slot_table(levels)[(side, level, r % HALF_LAT, place)]


def padded(count):
    return -(-count // 16) * 16


def send_gather(levels, row_count, even):
    half = levels // 2
    mine, theirs = (0, half) if even else (half, 0)
    parts = []
    for base, low, high in (
        (theirs, HALF_LAT, row_count),
        (mine, row_count, row_count + HALF_LAT),
        (theirs, row_count, row_count + HALF_LAT),
    ):
        rows = [
            coarse_slot(levels, even, r, base + e, c)
            for r in range(low, high)
            for e in range(half)
            for c in range(HALF_LON)
        ]
        parts += rows + [-1] * (padded(len(rows)) - len(rows))
    return column(parts)


def place_gather(levels, row_count, even):
    half = levels // 2
    out = np.full((4, row_count, WLON, half), -1)
    base = 0 if even else half
    for r in range(row_count):
        for e in range(half):
            for c in range(HALF_LON):
                mine, theirs = (c, c + HALF_LON) if even else (c + HALF_LON, c)
                if r >= HALF_LAT:
                    out[0, r, mine, e] = coarse_slot(levels, even, r, base + e, c)
                    out[1, r, theirs, e] = ((r - HALF_LAT) * half + e) * HALF_LON + c
                else:
                    out[2, r, mine, e] = (r * half + e) * HALF_LON + c
                    out[3, r, theirs, e] = (r * half + e) * HALF_LON + c
    return out.reshape(4, -1, 1).astype(np.int32)


def open_tables(levels):
    order = rolled_levels(levels)
    sides = np.arange(GROUP) // PART
    levs = np.arange(GROUP) % PART // HALF_LON % WLEV
    out = np.zeros((levels // WLEV, 2, GROUP, GROUP), np.float32)
    for pair in range(levels // WLEV):
        wrapped = np.asarray([order[pair * WLEV + v] < WLEV // 2 for v in range(WLEV)])[levs]
        seen = wrapped[:, None] == wrapped[None]
        out[pair, 0] = seen
        out[pair, 1] = seen & (sides[:, None] == sides[None])
    return np.tile(out, (1, 1, 2, 2))


PATCH, PICK, EDGE, COARSE, SEND, PLACE = 0, 1, 3, 5, 8, 10


def index_table(levels, row_count):
    half_rows = row_count // 2
    columns = [patch_gather(levels, row_count), *fine_gather(levels), *edge_gather(levels)]
    columns += [*coarse_gather(levels, half_rows)]
    columns += [send_gather(levels, half_rows, even) for even in (False, True)]
    for even in (False, True):
        columns += [*place_gather(levels, half_rows, even)]
    out = np.full((padded(max(len(c) for c in columns)), len(columns)), -(1 << 20), np.int32)
    for at, values in enumerate(columns):
        out[: len(values), at] = values[:, 0]
    return out


def column_of(table_ref, at, rows):
    return table_ref[rows, at : at + 1]


def parity_column(table_ref, at, step, even, rows):
    chosen = column_of(table_ref, at + step, rows), column_of(table_ref, at, rows)
    return jnp.where(even == 1, *chosen)


def one_hot(index, width):
    lanes = lax.broadcasted_iota(jnp.int32, (index.shape[0], width), 1)
    return (lanes == index).astype(jnp.float32).astype(jnp.bfloat16)


def mm(a, b):
    return jnp.dot(a, b, preferred_element_type=jnp.float32)


def layer_norm(values, norm_gain, offset):
    average = jnp.mean(values, axis=-1, keepdims=True)
    centred = values - average
    spread = jnp.mean(centred * centred, axis=-1, keepdims=True)
    return centred * lax.rsqrt(spread + norm_eps) * norm_gain + offset


def staged(tasks, stages):
    held = {}
    for step in range(len(tasks) + len(stages) - 1):
        for depth, stage in enumerate(stages):
            at = step - depth
            if 0 <= at < len(tasks):
                held[at] = stage(tasks[at], held.get(at))


def project(own, both, packed_ref, scale_ref, query, key, value):
    width = packed_ref.shape[1] // 3
    block = 2 * LANES
    rows = lax.broadcasted_iota(jnp.int32, (block, block), 0) // (LANES // 2)
    cols = lax.broadcasted_iota(jnp.int32, (block, block), 1) // (LANES // 2)
    same = (rows == cols).astype(jnp.float32).astype(jnp.bfloat16)
    lane = lax.broadcasted_iota(jnp.int32, (1, block), 1)
    first = (lane % LANES < LANES // 2).astype(jnp.float32)
    head = lane // (LANES // 2)
    half = both.shape[0] // 2
    tasks = []
    for j in range(width // block):
        tasks += [("q", 0, j), ("k", 0, j), ("k", 1, j), ("v", 0, j), ("v", 1, j)]

    def multiply(task, _):
        kind, part, j = task
        start = "qkv".index(kind) * width + j * block
        source = own[...] if kind == "q" else both[part * half : (part + 1) * half]
        return mm(source, packed_ref[:, start : start + block])

    def measure(task, rows):
        if task[0] == "v":
            return rows
        return rows, mm((rows * rows).astype(jnp.bfloat16), same)

    def keep(task, held):
        kind, part, j = task
        at = slice(j * block, (j + 1) * block)
        if kind == "v":
            value[part * half : (part + 1) * half, at] = held.astype(jnp.bfloat16)
            return
        rows, total = held
        rows = rows * lax.rsqrt(total + unit_eps)
        if kind == "k":
            key[part * half : (part + 1) * half, at] = rows.astype(jnp.bfloat16)
            return
        scale = jnp.zeros((1, block), jnp.float32)
        for h in range(2 * block // LANES):
            scale = jnp.where(head == h, scale_ref[j * 2 * block // LANES + h], scale)
        scale = scale * math.log2(math.e)
        left, right = rows * (scale * first), rows * (scale * (1.0 - first))
        for g in range(rows.shape[0] // GROUP):
            mine = slice(g * GROUP, (g + 1) * GROUP)
            query[2 * g * GROUP : 2 * (g + 1) * GROUP, at] = jnp.concatenate(
                [left[mine], right[mine]], axis=0
            ).astype(jnp.bfloat16)

    staged(tasks, [multiply, measure, keep])


def attend(wraps, query, key, value, open_ref, prob, ctx):
    width = query.shape[1]
    windows = len(wraps)
    pairs = query.shape[0] // windows // (2 * GROUP)
    is_first = lax.broadcasted_iota(jnp.int32, (GROUP, LANES), 1) < LANES // 2
    ones = jnp.ones((2 * GROUP, LANES), jnp.bfloat16)
    tasks = [
        (w, j, pair) for w in range(windows) for j in range(width // LANES) for pair in range(pairs)
    ]
    done = []

    def place(task):
        w, j, pair = task
        rows = slice((w * pairs + pair) * 2 * GROUP, (w * pairs + pair + 1) * 2 * GROUP)
        return rows, slice(j * LANES, (j + 1) * LANES), tasks.index(task) % prob.shape[0]

    def score(task, _):
        rows, at, slot = place(task)
        wrap, pair = wraps[task[0]], task[2]
        raw = lax.dot_general(
            query[rows, at],
            key[rows, at],
            (((1,), (1,)), ((), ())),
            preferred_element_type=jnp.float32,
        )
        raw = jnp.exp2(raw).astype(jnp.bfloat16)
        if wrap is not None or pair == pairs - 1:
            raw = raw * open_ref[pair, 0 if wrap is None else wrap]
        prob[slot] = raw

    def wait(task, _):
        return None

    def mix(task, _):
        rows, at, slot = place(task)
        out = mm(prob[slot], jnp.concatenate([value[rows, at], ones], axis=1))
        top = jnp.where(is_first, out[:GROUP, :LANES], out[GROUP:, :LANES])
        total = jnp.where(is_first, out[:GROUP, LANES:], out[GROUP:, LANES:])
        done.append(top / total)
        if len(done) == pairs:
            base = task[0] * pairs * GROUP
            ctx[base : base + pairs * GROUP, at] = jnp.concatenate(done, axis=0).astype(jnp.bfloat16)
            done.clear()

    staged(tasks, [score, wait, mix])


def attention_scratch(rows, width, depth):
    bf16 = jnp.bfloat16
    return [
        pltpu.VMEM((rows, depth), bf16),
        pltpu.VMEM((2 * rows, depth), bf16),
        pltpu.VMEM((2 * rows, width), bf16),
        pltpu.VMEM((2 * rows, width), bf16),
        pltpu.VMEM((2 * rows, width), bf16),
        pltpu.VMEM((8, 2 * GROUP, 2 * GROUP), bf16),
        pltpu.VMEM((rows, width), bf16),
    ]


def keep_window(w, mine, theirs, own, both):
    span = mine.shape[0]
    own[w * span : (w + 1) * span] = mine.astype(jnp.bfloat16)
    parts = []
    for at in range(0, span, GROUP):
        parts += [mine[at : at + GROUP], theirs[at : at + GROUP]]
    both[2 * w * span : 2 * (w + 1) * span] = jnp.concatenate(parts, axis=0).astype(jnp.bfloat16)


def block_rows(own, ctx, output_ref, gain_ref, offset_ref):
    branch = layer_norm(mm(ctx[...], output_ref[...]), gain_ref[...], offset_ref[...])
    return (own[...].astype(jnp.float32) + branch).astype(jnp.bfloat16)


def merge_rows(first, patch, merge_ref, gain_ref, offset_ref):
    cells = patch.shape[0] // 4
    channels = first.shape[1]
    part = mm(patch, first[...]).astype(jnp.bfloat16)
    total = None
    for g in range(4):
        term = mm(part[g * cells : (g + 1) * cells], merge_ref[g * channels : (g + 1) * channels])
        total = term if total is None else total + term
    return layer_norm(total, gain_ref[...], offset_ref[...]).astype(jnp.bfloat16)


def split_kernel(flags, grid_hbm, near_ref, far_ref, up_ref, down_ref, grid_ref, sem):
    fetch = pltpu.make_async_copy(grid_hbm, grid_ref, sem)
    fetch.start()
    levels, _, row_count, channels = grid_ref.shape
    lines = levels * HALF_LON
    chunks, tokens, _ = near_ref.shape
    place = lax.broadcasted_iota(jnp.int32, (row_count * lines, 1), 0)
    turn = one_hot(place % lines * row_count + place // lines, lines * row_count)
    fetch.wait()
    for side, dst in ((0, near_ref), (1, far_ref)):
        right = flags[2] if side == 0 else 1 - flags[2]
        half = grid_ref[:, pl.ds(right * HALF_LON, HALF_LON)].reshape(lines * row_count, channels)
        rows = mm(turn, half)
        for e in range(chunks):
            chunk = rows[e * tokens : (e + 1) * tokens].astype(jnp.bfloat16)
            dst[e] = chunk
            if e == 0:
                up_ref[side] = chunk
            if e == chunks - 1:
                down_ref[side] = chunk


def load_kernel(*refs):
    count = len(refs) // 2
    copies = [
        pltpu.make_async_copy(src, dst, refs[-1].at[i])
        for i, (src, dst) in enumerate(zip(refs[:count], refs[count:-1]))
    ]
    for copy in copies:
        copy.start()
    for copy in copies:
        copy.wait()


def first_windows(
    lines, wraps, table_ref, packed_ref, scale_ref, output_ref, gain_ref, offset_ref, open_ref, scratch
):
    own, both, query, key, value, prob, ctx = scratch
    tokens = lines[0][0].shape[0]
    span = open_ref.shape[0] * GROUP
    pick = [one_hot(column_of(table_ref, PICK + s, slice(0, span)), tokens) for s in range(2)]
    for w in range(len(wraps)):
        mine, theirs = (
            mm(pick[0], line[2 * w]) + mm(pick[1], line[2 * w + 1]) for line in lines
        )
        keep_window(w, mine, theirs, own, both)
    project(own, both, packed_ref, scale_ref, query, key, value)
    attend(wraps, query, key, value, open_ref, prob, ctx)
    return block_rows(own, ctx, output_ref, gain_ref, offset_ref)


def inner_kernel(
    scale_ref,
    own_ref,
    other_ref,
    packed_ref,
    output_ref,
    gain_ref,
    offset_ref,
    open_ref,
    table_ref,
    rows_ref,
    *scratch,
):
    chunks = own_ref.shape[0]
    lines = [[ref[e] for e in range(1, chunks - 1)] for ref in (own_ref, other_ref)]
    rows_ref[...] = first_windows(
        lines,
        [None] * (chunks // 2 - 1),
        table_ref,
        packed_ref,
        scale_ref,
        output_ref,
        gain_ref,
        offset_ref,
        open_ref,
        scratch,
    )


def side_kernel(
    scale_ref,
    flags,
    own_ref,
    other_ref,
    top_ref,
    bottom_ref,
    other_top_ref,
    other_bottom_ref,
    packed_ref,
    output_ref,
    gain_ref,
    offset_ref,
    merge_gain_ref,
    merge_offset_ref,
    open_ref,
    table_ref,
    merge_hbm,
    *rest,
):
    if len(rest) == 12:
        side, (inner_ref, merged_ref, *rest) = 0, rest
    else:
        side, (near_ref, merged_ref, up_ref, *rest) = 1, rest
    merge_ref, sem, first, *scratch = rest
    merge_copy = pltpu.make_async_copy(merge_hbm, merge_ref, sem)
    merge_copy.start()
    chunks = own_ref.shape[0]
    span = open_ref.shape[0] * GROUP
    inside = range(chunks) if side else (0, chunks - 1)
    lines = []
    for src, top, bottom in (
        (own_ref, top_ref[side], bottom_ref[side]),
        (other_ref, other_top_ref[0], other_bottom_ref[side]),
    ):
        lines.append([top] + [src[e] for e in inside] + [bottom])
    wraps = [flags[0]] + [None] * (len(inside) // 2 - 1) + [flags[1]]
    rows = first_windows(
        lines,
        wraps,
        table_ref,
        packed_ref,
        scale_ref,
        output_ref,
        gain_ref,
        offset_ref,
        open_ref,
        scratch,
    )
    if side:
        first[...] = rows
    else:
        first[:span] = rows[:span]
        first[span : first.shape[0] - span] = inner_ref[...]
        first[first.shape[0] - span :] = rows[span:]
    merge_copy.wait()
    cells = 4 * merged_ref.shape[0]
    patch = one_hot(column_of(table_ref, PATCH, slice(0, cells)), first.shape[0])
    merged = merge_rows(first, patch, merge_ref, merge_gain_ref, merge_offset_ref)
    merged_ref[...] = merged
    if side:
        count = up_ref.shape[0]
        reach = padded(count // 2)
        up_ref[...] = sum(
            mm(one_hot(column_of(table_ref, EDGE + s, slice(0, count)), reach), rows[:reach])
            for s, rows in enumerate((near_ref, merged))
        ).astype(jnp.bfloat16)


def coarse_rows(w, span, near_ref, far_ref, rim_ref, table_ref, last):
    small = rim_ref.shape[0] // 2
    low, high = coarse_reach(w, small, near_ref.shape[0])
    reach = [(0, low, high), (1, low, high)] + ([(2, 0, 2 * small)] if last else [])
    rows = 0.0
    for s, low, high in reach:
        index = column_of(table_ref, COARSE + s, slice(w * span, (w + 1) * span))
        rows += mm(one_hot(index, high - low), (near_ref, far_ref, rim_ref)[s][low:high])
    return rows


def head_sums():
    block = 2 * LANES
    rows = lax.broadcasted_iota(jnp.int32, (block, block), 0) // (LANES // 2)
    cols = lax.broadcasted_iota(jnp.int32, (block, block), 1) // (LANES // 2)
    return (rows == cols).astype(jnp.float32).astype(jnp.bfloat16)


def mine_kernel(
    span,
    scale_ref,
    near_ref,
    far_ref,
    rim_ref,
    packed_ref,
    table_ref,
    own_ref,
    query_ref,
    key_ref,
    value_ref,
):
    windows = own_ref.shape[0] // span
    for w in range(windows):
        rows = coarse_rows(w, span, near_ref, far_ref, rim_ref, table_ref, w == windows - 1)
        own_ref[w * span : (w + 1) * span] = rows.astype(jnp.bfloat16)
    width = key_ref.shape[1]
    block = 2 * LANES
    same = head_sums()
    lane = lax.broadcasted_iota(jnp.int32, (1, block), 1)
    first = (lane % LANES < LANES // 2).astype(jnp.float32)
    head = lane // (LANES // 2)

    def multiply(task, _):
        start = "qkv".index(task[0]) * width + task[1] * block
        return mm(own_ref[...], packed_ref[:, start : start + block])

    def measure(task, rows):
        return rows, None if task[0] == "v" else mm((rows * rows).astype(jnp.bfloat16), same)

    def keep(task, held):
        kind, j = task
        rows, total = held
        at = slice(j * block, (j + 1) * block)
        if kind == "v":
            value_ref[:, at] = rows
            return
        rows = rows * lax.rsqrt(total + unit_eps)
        if kind == "k":
            key_ref[:, at] = rows
            return
        scale = jnp.zeros((1, block), jnp.float32)
        for h in range(2 * block // LANES):
            scale = jnp.where(head == h, scale_ref[j * 2 * block // LANES + h], scale)
        scale = scale * math.log2(math.e)
        left, right = rows * (scale * first), rows * (scale * (1.0 - first))
        for g in range(rows.shape[0] // GROUP):
            mine = slice(g * GROUP, (g + 1) * GROUP)
            query_ref[2 * g * GROUP : 2 * (g + 1) * GROUP, at] = jnp.concatenate(
                [left[mine], right[mine]], axis=0
            ).astype(jnp.bfloat16)

    staged([(k, j) for j in range(width // block) for k in "qkv"], [multiply, measure, keep])


def second_kernel(
    flags,
    own_ref,
    query_ref,
    own_key_ref,
    own_value_ref,
    other_near_ref,
    other_far_ref,
    other_rim_ref,
    packed_ref,
    output_ref,
    gain_ref,
    offset_ref,
    open_ref,
    table_ref,
    second_ref,
    send_ref,
    return_ref,
    return_near_ref,
    other,
    key,
    value,
    prob,
    ctx,
):
    span = open_ref.shape[0] * GROUP
    windows = own_ref.shape[0] // span
    for w in range(windows):
        rows = coarse_rows(
            w, span, other_near_ref, other_far_ref, other_rim_ref, table_ref, w == windows - 1
        )
        other[w * span : (w + 1) * span] = rows.astype(jnp.bfloat16)
    width = own_key_ref.shape[1]
    block = 2 * LANES
    same = head_sums()

    def multiply(task, _):
        start = "qkv".index(task[0]) * width + task[1] * block
        return mm(other[...], packed_ref[:, start : start + block])

    def measure(task, rows):
        return rows, None if task[0] == "v" else mm((rows * rows).astype(jnp.bfloat16), same)

    def keep(task, held):
        kind, j = task
        rows, total = held
        at = slice(j * block, (j + 1) * block)
        if kind == "k":
            rows = rows * lax.rsqrt(total + unit_eps)
        source, dst = (own_key_ref, key) if kind == "k" else (own_value_ref, value)
        for g in range(rows.shape[0] // GROUP):
            mine = slice(g * GROUP, (g + 1) * GROUP)
            dst[2 * g * GROUP : 2 * (g + 1) * GROUP, at] = jnp.concatenate(
                [source[mine, at], rows[mine]], axis=0
            ).astype(jnp.bfloat16)

    staged([(k, j) for j in range(width // block) for k in "kv"], [multiply, measure, keep])
    attend([None] * (windows - 1) + [flags[1]], query_ref, key, value, open_ref, prob, ctx)
    second = block_rows(own_ref, ctx, output_ref, gain_ref, offset_ref)
    second_ref[...] = second
    counts = [padded(ref.shape[0]) for ref in (send_ref, return_ref, return_near_ref)]
    index = parity_column(table_ref, SEND, 1, flags[2], slice(0, sum(counts)))
    rows = mm(one_hot(index, second.shape[0]), second).astype(jnp.bfloat16)
    at = 0
    for dst in (send_ref, return_ref, return_near_ref):
        count = dst.shape[0]
        dst[...] = rows[at : at + count]
        at += padded(count)


def place(pieces, out_ref, rows_ref, sem, low):
    rows, _, columns, pair, _ = rows_ref.shape
    block = sum(mm(one_hot(index, ref.shape[0]), ref[...]) for index, ref in pieces)
    for r in range(rows):
        for c in range(columns):
            at = (r * columns + c) * pair
            rows_ref[r, 0, c] = block[at : at + pair].astype(jnp.bfloat16)
    copy = pltpu.make_async_copy(rows_ref, out_ref.at[low : low + rows], sem)
    copy.start()
    copy.wait()


def place_columns(flags, table_ref, out_ref, which, early):
    step = out_ref.shape[2] * out_ref.shape[3]
    edge = HALF_LAT * step
    rows = slice(0, edge) if early else slice(edge, step * out_ref.shape[0])
    return [parity_column(table_ref, PLACE + s, 4, flags[2], rows) for s in which]


def late_kernel(flags, second_ref, near_ref, table_ref, out_ref, rows_ref, sem):
    index = place_columns(flags, table_ref, out_ref, (0, 1), False)
    place(zip(index, (second_ref, near_ref)), out_ref, rows_ref, sem, HALF_LAT)


def early_kernel(flags, back_ref, back_near_ref, table_ref, _, out_ref, rows_ref, sem):
    index = place_columns(flags, table_ref, out_ref, (2, 3), True)
    place(zip(index, (back_ref, back_near_ref)), out_ref, rows_ref, sem, 0)


def in_hbm(value):
    return pltpu.with_memory_space_constraint(value, pltpu.HBM)


def call(
    kernel, outs, scratch, scalars, operands, fixed=(), late=(), alias=None, held=False, room=SECOND_BYTES
):
    vmem = pl.BlockSpec(memory_space=pltpu.VMEM)
    hbm = pl.BlockSpec(memory_space=pltpu.HBM)
    fixed = [in_hbm(x) for x in fixed]
    return pl.pallas_call(
        kernel,
        out_shape=outs,
        in_specs=[pl.BlockSpec(memory_space=pltpu.SMEM)] * len(scalars)
        + [vmem] * len(operands)
        + [hbm] * len(fixed)
        + [vmem] * len(late),
        out_specs=[hbm if held else vmem] * len(outs),
        scratch_shapes=scratch,
        input_output_aliases=alias or {},
        compiler_params=pltpu.CompilerParams(vmem_limit_bytes=room),
    )(*scalars, *operands, *fixed, *late)


def far_of(i, n):
    return (i + (1 if i % 2 else -1)) % n


def near_swap(value):
    return lax.ppermute(value, "lon", [(i, i ^ 1) for i in range(lax.axis_size("lon"))])


def far_swap(value):
    n = lax.axis_size("lon")
    return lax.ppermute(value, "lon", [(i, far_of(i, n)) for i in range(n)])


def ring(value, by, turn):
    n, m = lax.axis_size("lat"), lax.axis_size("lon")
    links = [(i * m + j, (i + by) % n * m + turn(j, m)) for i in range(n) for j in range(m)]
    return lax.ppermute(value, ("lat", "lon"), links)


def shift(value, by):
    n = lax.axis_size("lat")
    return lax.ppermute(value, "lat", [(i, i + by) for i in range(n) if 0 <= i + by < n])


def body(
    features,
    packed_first,
    scale_first,
    output_first,
    gain_first,
    offset_first,
    merge_weight,
    merge_gain,
    merge_offset,
    packed_second,
    scale_second,
    output_second,
    gain_second,
    offset_second,
):
    levels, row_count, col_count, channels = features.shape
    inner = packed_first.shape[1] // 3
    second_inner = packed_second.shape[1] // 3
    wide = merge_weight.shape[1]
    half_rows = row_count // 2
    lat_pos = lax.axis_index("lat")
    odd = lax.axis_index("lon") % 2
    last = lax.axis_size("lat") - 1
    place = jnp.stack([lat_pos, lat_pos, 1 - odd])
    flags = (place == jnp.asarray([0, last, 1], jnp.int32)).astype(jnp.int32)
    bf16 = jnp.bfloat16
    span = levels // WLEV * GROUP
    tokens = HALF_LAT * levels * HALF_LON
    chunks = row_count // HALF_LAT
    windows = chunks // 2 + 1

    half = jax.ShapeDtypeStruct((chunks, tokens, channels), bf16)
    ends = jax.ShapeDtypeStruct((2, tokens, channels), bf16)
    near, far, ups, downs = call(
        split_kernel,
        [half, half, ends, ends],
        [pltpu.VMEM((levels, col_count, row_count, channels), bf16), pltpu.SemaphoreType.DMA],
        [flags],
        [],
        [jnp.transpose(features, (0, 2, 1, 3))],
    )
    bottom = shift(ups, -1)
    top = shift(downs, 1)
    near_other = near_swap(near)
    far_other = far_swap(far)
    near_other_top, near_other_bottom = near_swap(top), near_swap(bottom)
    far_rim = far_swap(jnp.stack([top[1], bottom[1]]))

    opened = jnp.asarray(open_tables(levels), bf16)
    cells = half_rows * levels * HALF_LON // 2
    small = jax.ShapeDtypeStruct((cells, wide), bf16)
    edge = jax.ShapeDtypeStruct((tokens, wide), bf16)

    shared = [packed_first, output_first, gain_first[None], offset_first[None]]
    shared += [merge_gain[None], merge_offset[None], opened]
    shared += [jnp.asarray(index_table(levels, row_count))]
    shared = call(
        load_kernel,
        [jax.ShapeDtypeStruct(x.shape, x.dtype) for x in shared],
        [pltpu.SemaphoreType.DMA((len(shared),))],
        [],
        [],
        shared,
    )
    shared = list(shared)
    opened, table = shared[-2:]
    buffers = [pltpu.VMEM(merge_weight.shape, bf16), pltpu.SemaphoreType.DMA]
    buffers += [pltpu.VMEM((windows * span, channels), bf16)]
    (inner_rows,) = call(
        inner_kernel,
        [jax.ShapeDtypeStruct(((windows - 2) * span, channels), bf16)],
        attention_scratch((windows - 2) * span, inner, channels),
        [in_hbm(scale_first)],
        [near, near_other] + shared[:4] + shared[-2:],
    )
    (merged_near,) = call(
        side_kernel,
        [small],
        buffers + attention_scratch(2 * span, inner, channels),
        [in_hbm(scale_first), flags],
        [near, near_other, top, bottom, near_other_top, near_other_bottom] + shared,
        [merge_weight],
        [inner_rows],
        room=FIRST_BYTES,
    )
    other_near = far_swap(merged_near)
    merged_far, edge_up = call(
        side_kernel,
        [small, edge],
        buffers + attention_scratch(windows * span, inner, channels),
        [in_hbm(scale_first), flags],
        [far, far_other, top, bottom, far_rim, far_rim] + shared,
        [merge_weight],
        [merged_near],
        room=FIRST_BYTES,
    )
    other_far = far_swap(merged_far)
    other_rim = ring(edge_up, -1, far_of)
    rim = ring(edge_up, -1, lambda j, m: j)

    windows = half_rows // WLAT
    share = levels // 2 * HALF_LON

    back = jax.ShapeDtypeStruct((HALF_LAT * share, wide), bf16)
    rows = windows * span
    mine = call(
        functools.partial(mine_kernel, span),
        [
            jax.ShapeDtypeStruct((rows, wide), bf16),
            jax.ShapeDtypeStruct((2 * rows, second_inner), bf16),
            jax.ShapeDtypeStruct((rows, second_inner), jnp.float32),
            jax.ShapeDtypeStruct((rows, second_inner), jnp.float32),
        ],
        [],
        [in_hbm(scale_second)],
        [merged_near, merged_far, rim, packed_second, table],
    )
    second, send, back_same, back_near = call(
        second_kernel,
        [
            jax.ShapeDtypeStruct((windows * span, wide), bf16),
            jax.ShapeDtypeStruct(((half_rows - HALF_LAT) * share, wide), bf16),
            back,
            back,
        ],
        [pltpu.VMEM((rows, wide), bf16)] + attention_scratch(rows, second_inner, wide)[3:],
        [flags],
        [
            *mine,
            other_near,
            other_far,
            other_rim,
            packed_second,
            output_second,
            gain_second[None],
            offset_second[None],
            opened,
            table,
        ],
    )
    back_near = ring(back_near, 1, lambda j, m: j ^ 1)
    back_same = ring(back_same, 1, lambda j, m: j)
    received = near_swap(send)
    shape = (half_rows, 1, WLON, levels // 2, wide)
    whole = [jax.ShapeDtypeStruct(shape, bf16)]

    def room(rows):
        return [pltpu.VMEM((rows,) + shape[1:], bf16), pltpu.SemaphoreType.DMA]

    (out,) = call(
        late_kernel,
        whole,
        room(half_rows - HALF_LAT),
        [flags],
        [second, received, table],
        held=True,
    )
    (out,) = call(
        early_kernel,
        whole,
        room(HALF_LAT),
        [flags],
        [back_same, back_near, table],
        [out],
        alias={4: 0},
        held=True,
    )
    return jnp.transpose(out, (0, 1, 3, 2, 4))


def solution(mesh):
    return jax.shard_map(
        body,
        mesh=mesh,
        in_specs=(P(None, "lat", "lon", None),) + (P(),) * 13,
        out_specs=P("lat", "lon", None, None, None),
        check_vma=False,
    )
```

```python
import functools
import math

import jax
import jax.numpy as jnp
import numpy as np
from jax import lax
from jax.experimental import pallas as pl
from jax.experimental.pallas import tpu as pltpu
from jax.sharding import PartitionSpec as P

WLEV = 2
WLAT = 6
WLON = 12
HALF_LAT = WLAT // 2
HALF_LON = WLON // 2
LANES = 128
FIRST_BYTES, SECOND_BYTES = 48 << 20, 32 << 20

norm_eps = 1e-05
unit_eps = 1e-06

PART = WLEV * HALF_LAT * HALF_LON
GROUP = 2 * PART


def rolled_levels(levels):
    return [(l + WLEV // 2) % levels for l in range(levels)]


def window_slots(levels):
    order = rolled_levels(levels)
    for place, level in enumerate(order):
        pair, lev = divmod(place, WLEV)
        for side in range(2):
            for i in range(HALF_LAT):
                for c in range(HALF_LON):
                    t = (i * WLEV + lev) * HALF_LON + c
                    yield pair * GROUP + side * PART + t, side, level, i, c


def slot_table(levels):
    table = {}
    for row, side, level, i, c in window_slots(levels):
        table[(side, level, i, c)] = row
    return table


def column(values):
    return np.asarray(values, np.int32).reshape(-1, 1)


def fine_gather(levels):
    rows = levels // WLEV * GROUP
    out = [np.full(rows, -1), np.full(rows, -1)]
    for row, side, level, i, c in window_slots(levels):
        out[side][row] = (i * levels + level) * HALF_LON + c
    return column(out[0]), column(out[1])


def patch_gather(levels, row_count):
    span = levels // WLEV * GROUP
    slots = slot_table(levels)
    out = []
    for g in range(4):
        dc, dr = divmod(g, 2)
        rows = []
        for i in range(row_count // 2):
            for level in range(levels):
                for cc in range(HALF_LON // 2):
                    r = 2 * i + dr
                    chunk = r // HALF_LAT + 1
                    w, side = divmod(chunk, 2)
                    rows.append(w * span + slots[(side, level, r % HALF_LAT, 2 * cc + dc)])
        out.append(column(rows))
    return np.concatenate(out)


def coarse_gather(levels, row_count):
    span = levels // WLEV * GROUP
    chunks = row_count // HALF_LAT
    third = HALF_LON // 2
    small = HALF_LAT * levels * third
    out = np.full((3, chunks // 2 * span, 1), -(1 << 20), np.int32)
    for w in range(chunks // 2):
        for row, side, level, i, c in window_slots(levels):
            chunk = 2 * w + side + 1
            which, cc = divmod(c, third)
            cell = (i * levels + level) * third + cc
            at = w * span + row
            if chunk < chunks:
                low = coarse_reach(w, small, chunks * small)[0]
                out[which, at, 0] = chunk * small + cell - low
            else:
                out[2, at, 0] = which * small + cell
    return out


def coarse_reach(w, small, count):
    return (2 * w + 1) * small // 16 * 16, min(padded((2 * w + 3) * small), count)


def edge_gather(levels):
    small = HALF_LAT * levels * HALF_LON // 2
    out = np.full((2, 2 * small, 1), -1, np.int32)
    for which in range(2):
        out[which, which * small : (which + 1) * small, 0] = np.arange(small)
    return out


def coarse_slot(levels, even, r, level, c):
    third = HALF_LON // 2
    place = (c + third) % HALF_LON if even else c
    w, side = divmod(r // HALF_LAT - 1, 2)
    return w * (levels // WLEV * GROUP) + slot_table(levels)[(side, level, r % HALF_LAT, place)]


def padded(count):
    return -(-count // 16) * 16


def send_gather(levels, row_count, even):
    half = levels // 2
    mine, theirs = (0, half) if even else (half, 0)
    parts = []
    for base, low, high in (
        (theirs, HALF_LAT, row_count),
        (mine, row_count, row_count + HALF_LAT),
        (theirs, row_count, row_count + HALF_LAT),
    ):
        rows = [
            coarse_slot(levels, even, r, base + e, c)
            for r in range(low, high)
            for e in range(half)
            for c in range(HALF_LON)
        ]
        parts += rows + [-1] * (padded(len(rows)) - len(rows))
    return column(parts)


def place_gather(levels, row_count, even):
    half = levels // 2
    out = np.full((4, row_count, WLON, half), -1)
    base = 0 if even else half
    for r in range(row_count):
        for e in range(half):
            for c in range(HALF_LON):
                mine, theirs = (c, c + HALF_LON) if even else (c + HALF_LON, c)
                if r >= HALF_LAT:
                    out[0, r, mine, e] = coarse_slot(levels, even, r, base + e, c)
                    out[1, r, theirs, e] = ((r - HALF_LAT) * half + e) * HALF_LON + c
                else:
                    out[2, r, mine, e] = (r * half + e) * HALF_LON + c
                    out[3, r, theirs, e] = (r * half + e) * HALF_LON + c
    return out.reshape(4, -1, 1).astype(np.int32)


def open_tables(levels):
    order = rolled_levels(levels)
    sides = np.arange(GROUP) // PART
    levs = np.arange(GROUP) % PART // HALF_LON % WLEV
    out = np.zeros((levels // WLEV, 2, GROUP, GROUP), np.float32)
    for pair in range(levels // WLEV):
        wrapped = np.asarray([order[pair * WLEV + v] < WLEV // 2 for v in range(WLEV)])[levs]
        seen = wrapped[:, None] == wrapped[None]
        out[pair, 0] = seen
        out[pair, 1] = seen & (sides[:, None] == sides[None])
    return np.tile(out, (1, 1, 2, 2))


PATCH, PICK, EDGE, COARSE, SEND, PLACE = 0, 1, 3, 5, 8, 10


def index_table(levels, row_count):
    half_rows = row_count // 2
    columns = [patch_gather(levels, row_count), *fine_gather(levels), *edge_gather(levels)]
    columns += [*coarse_gather(levels, half_rows)]
    columns += [send_gather(levels, half_rows, even) for even in (False, True)]
    for even in (False, True):
        columns += [*place_gather(levels, half_rows, even)]
    out = np.full((padded(max(len(c) for c in columns)), len(columns)), -(1 << 20), np.int32)
    for at, values in enumerate(columns):
        out[: len(values), at] = values[:, 0]
    return out


def column_of(table_ref, at, rows):
    return table_ref[rows, at : at + 1]


def parity_column(table_ref, at, step, even, rows):
    chosen = column_of(table_ref, at + step, rows), column_of(table_ref, at, rows)
    return jnp.where(even == 1, *chosen)


def one_hot(index, width):
    lanes = lax.broadcasted_iota(jnp.int32, (index.shape[0], width), 1)
    return (lanes == index).astype(jnp.float32).astype(jnp.bfloat16)


def mm(a, b):
    return jnp.dot(a, b, preferred_element_type=jnp.float32)


def layer_norm(values, norm_gain, offset):
    average = jnp.mean(values, axis=-1, keepdims=True)
    centred = values - average
    spread = jnp.mean(centred * centred, axis=-1, keepdims=True)
    return centred * lax.rsqrt(spread + norm_eps) * norm_gain + offset


def staged(tasks, stages):
    held = {}
    for step in range(len(tasks) + len(stages) - 1):
        for depth, stage in enumerate(stages):
            at = step - depth
            if 0 <= at < len(tasks):
                held[at] = stage(tasks[at], held.get(at))


def project(own, both, packed_ref, scale_ref, query, key, value):
    width = packed_ref.shape[1] // 3
    block = 2 * LANES
    rows = lax.broadcasted_iota(jnp.int32, (block, block), 0) // (LANES // 2)
    cols = lax.broadcasted_iota(jnp.int32, (block, block), 1) // (LANES // 2)
    same = (rows == cols).astype(jnp.float32).astype(jnp.bfloat16)
    lane = lax.broadcasted_iota(jnp.int32, (1, block), 1)
    first = (lane % LANES < LANES // 2).astype(jnp.float32)
    head = lane // (LANES // 2)
    half = both.shape[0] // 2
    tasks = []
    for j in range(width // block):
        tasks += [("q", 0, j), ("k", 0, j), ("k", 1, j), ("v", 0, j), ("v", 1, j)]

    def multiply(task, _):
        kind, part, j = task
        start = "qkv".index(kind) * width + j * block
        source = own[...] if kind == "q" else both[part * half : (part + 1) * half]
        return mm(source, packed_ref[:, start : start + block])

    def measure(task, rows):
        if task[0] == "v":
            return rows
        return rows, mm((rows * rows).astype(jnp.bfloat16), same)

    def keep(task, held):
        kind, part, j = task
        at = slice(j * block, (j + 1) * block)
        if kind == "v":
            value[part * half : (part + 1) * half, at] = held.astype(jnp.bfloat16)
            return
        rows, total = held
        rows = rows * lax.rsqrt(total + unit_eps)
        if kind == "k":
            key[part * half : (part + 1) * half, at] = rows.astype(jnp.bfloat16)
            return
        scale = jnp.zeros((1, block), jnp.float32)
        for h in range(2 * block // LANES):
            scale = jnp.where(head == h, scale_ref[j * 2 * block // LANES + h], scale)
        scale = scale * math.log2(math.e)
        left, right = rows * (scale * first), rows * (scale * (1.0 - first))
        for g in range(rows.shape[0] // GROUP):
            mine = slice(g * GROUP, (g + 1) * GROUP)
            query[2 * g * GROUP : 2 * (g + 1) * GROUP, at] = jnp.concatenate(
                [left[mine], right[mine]], axis=0
            ).astype(jnp.bfloat16)

    staged(tasks, [multiply, measure, keep])


def attend(wraps, query, key, value, open_ref, prob, ctx):
    width = query.shape[1]
    windows = len(wraps)
    pairs = query.shape[0] // windows // (2 * GROUP)
    is_first = lax.broadcasted_iota(jnp.int32, (GROUP, LANES), 1) < LANES // 2
    ones = jnp.ones((2 * GROUP, LANES), jnp.bfloat16)
    tasks = [
        (w, j, pair) for w in range(windows) for j in range(width // LANES) for pair in range(pairs)
    ]
    done = []

    def place(task):
        w, j, pair = task
        rows = slice((w * pairs + pair) * 2 * GROUP, (w * pairs + pair + 1) * 2 * GROUP)
        return rows, slice(j * LANES, (j + 1) * LANES), tasks.index(task) % prob.shape[0]

    def score(task, _):
        rows, at, slot = place(task)
        wrap, pair = wraps[task[0]], task[2]
        raw = lax.dot_general(
            query[rows, at],
            key[rows, at],
            (((1,), (1,)), ((), ())),
            preferred_element_type=jnp.float32,
        )
        raw = jnp.exp2(raw).astype(jnp.bfloat16)
        if wrap is not None or pair == pairs - 1:
            raw = raw * open_ref[pair, 0 if wrap is None else wrap]
        prob[slot] = raw

    def wait(task, _):
        return None

    def mix(task, _):
        rows, at, slot = place(task)
        out = mm(prob[slot], jnp.concatenate([value[rows, at], ones], axis=1))
        top = jnp.where(is_first, out[:GROUP, :LANES], out[GROUP:, :LANES])
        total = jnp.where(is_first, out[:GROUP, LANES:], out[GROUP:, LANES:])
        done.append(top / total)
        if len(done) == pairs:
            base = task[0] * pairs * GROUP
            ctx[base : base + pairs * GROUP, at] = jnp.concatenate(done, axis=0).astype(jnp.bfloat16)
            done.clear()

    staged(tasks, [score, wait, mix])


def attention_scratch(rows, width, depth):
    bf16 = jnp.bfloat16
    return [
        pltpu.VMEM((rows, depth), bf16),
        pltpu.VMEM((2 * rows, depth), bf16),
        pltpu.VMEM((2 * rows, width), bf16),
        pltpu.VMEM((2 * rows, width), bf16),
        pltpu.VMEM((2 * rows, width), bf16),
        pltpu.VMEM((8, 2 * GROUP, 2 * GROUP), bf16),
        pltpu.VMEM((rows, width), bf16),
    ]


def keep_window(w, mine, theirs, own, both):
    span = mine.shape[0]
    own[w * span : (w + 1) * span] = mine.astype(jnp.bfloat16)
    parts = []
    for at in range(0, span, GROUP):
        parts += [mine[at : at + GROUP], theirs[at : at + GROUP]]
    both[2 * w * span : 2 * (w + 1) * span] = jnp.concatenate(parts, axis=0).astype(jnp.bfloat16)


def block_rows(own, ctx, output_ref, gain_ref, offset_ref):
    branch = layer_norm(mm(ctx[...], output_ref[...]), gain_ref[...], offset_ref[...])
    return (own[...].astype(jnp.float32) + branch).astype(jnp.bfloat16)


def merge_rows(first, patch, merge_ref, gain_ref, offset_ref):
    cells = patch.shape[0] // 4
    channels = first.shape[1]
    part = mm(patch, first[...]).astype(jnp.bfloat16)
    total = None
    for g in range(4):
        term = mm(part[g * cells : (g + 1) * cells], merge_ref[g * channels : (g + 1) * channels])
        total = term if total is None else total + term
    return layer_norm(total, gain_ref[...], offset_ref[...]).astype(jnp.bfloat16)


def split_kernel(flags, grid_hbm, near_ref, far_ref, up_ref, down_ref, grid_ref, sem):
    fetch = pltpu.make_async_copy(grid_hbm, grid_ref, sem)
    fetch.start()
    levels, _, row_count, channels = grid_ref.shape
    lines = levels * HALF_LON
    chunks, tokens, _ = near_ref.shape
    place = lax.broadcasted_iota(jnp.int32, (row_count * lines, 1), 0)
    turn = one_hot(place % lines * row_count + place // lines, lines * row_count)
    fetch.wait()
    for side, dst in ((0, near_ref), (1, far_ref)):
        right = flags[2] if side == 0 else 1 - flags[2]
        half = grid_ref[:, pl.ds(right * HALF_LON, HALF_LON)].reshape(lines * row_count, channels)
        rows = mm(turn, half)
        for e in range(chunks):
            chunk = rows[e * tokens : (e + 1) * tokens].astype(jnp.bfloat16)
            dst[e] = chunk
            if e == 0:
                up_ref[side] = chunk
            if e == chunks - 1:
                down_ref[side] = chunk


def load_kernel(*refs):
    count = len(refs) // 2
    copies = [
        pltpu.make_async_copy(src, dst, refs[-1].at[i])
        for i, (src, dst) in enumerate(zip(refs[:count], refs[count:-1]))
    ]
    for copy in copies:
        copy.start()
    for copy in copies:
        copy.wait()


def first_windows(
    lines, wraps, table_ref, packed_ref, scale_ref, output_ref, gain_ref, offset_ref, open_ref, scratch
):
    own, both, query, key, value, prob, ctx = scratch
    tokens = lines[0][0].shape[0]
    span = open_ref.shape[0] * GROUP
    pick = [one_hot(column_of(table_ref, PICK + s, slice(0, span)), tokens) for s in range(2)]
    for w in range(len(wraps)):
        mine, theirs = (
            mm(pick[0], line[2 * w]) + mm(pick[1], line[2 * w + 1]) for line in lines
        )
        keep_window(w, mine, theirs, own, both)
    project(own, both, packed_ref, scale_ref, query, key, value)
    attend(wraps, query, key, value, open_ref, prob, ctx)
    return block_rows(own, ctx, output_ref, gain_ref, offset_ref)


def inner_kernel(
    scale_ref,
    own_ref,
    other_ref,
    packed_ref,
    output_ref,
    gain_ref,
    offset_ref,
    open_ref,
    table_ref,
    rows_ref,
    *scratch,
):
    chunks = own_ref.shape[0]
    lines = [[ref[e] for e in range(1, chunks - 1)] for ref in (own_ref, other_ref)]
    rows_ref[...] = first_windows(
        lines,
        [None] * (chunks // 2 - 1),
        table_ref,
        packed_ref,
        scale_ref,
        output_ref,
        gain_ref,
        offset_ref,
        open_ref,
        scratch,
    )


def side_kernel(
    scale_ref,
    flags,
    own_ref,
    other_ref,
    top_ref,
    bottom_ref,
    other_top_ref,
    other_bottom_ref,
    packed_ref,
    output_ref,
    gain_ref,
    offset_ref,
    merge_gain_ref,
    merge_offset_ref,
    open_ref,
    table_ref,
    merge_hbm,
    *rest,
):
    if len(rest) == 12:
        side, (inner_ref, merged_ref, *rest) = 0, rest
    else:
        side, (near_ref, merged_ref, up_ref, *rest) = 1, rest
    merge_ref, sem, first, *scratch = rest
    merge_copy = pltpu.make_async_copy(merge_hbm, merge_ref, sem)
    merge_copy.start()
    chunks = own_ref.shape[0]
    span = open_ref.shape[0] * GROUP
    inside = range(chunks) if side else (0, chunks - 1)
    lines = []
    for src, top, bottom in (
        (own_ref, top_ref[side], bottom_ref[side]),
        (other_ref, other_top_ref[0], other_bottom_ref[side]),
    ):
        lines.append([top] + [src[e] for e in inside] + [bottom])
    wraps = [flags[0]] + [None] * (len(inside) // 2 - 1) + [flags[1]]
    rows = first_windows(
        lines,
        wraps,
        table_ref,
        packed_ref,
        scale_ref,
        output_ref,
        gain_ref,
        offset_ref,
        open_ref,
        scratch,
    )
    if side:
        first[...] = rows
    else:
        first[:span] = rows[:span]
        first[span : first.shape[0] - span] = inner_ref[...]
        first[first.shape[0] - span :] = rows[span:]
    merge_copy.wait()
    cells = 4 * merged_ref.shape[0]
    patch = one_hot(column_of(table_ref, PATCH, slice(0, cells)), first.shape[0])
    merged = merge_rows(first, patch, merge_ref, merge_gain_ref, merge_offset_ref)
    merged_ref[...] = merged
    if side:
        count = up_ref.shape[0]
        reach = padded(count // 2)
        up_ref[...] = sum(
            mm(one_hot(column_of(table_ref, EDGE + s, slice(0, count)), reach), rows[:reach])
            for s, rows in enumerate((near_ref, merged))
        ).astype(jnp.bfloat16)


def coarse_rows(w, span, near_ref, far_ref, rim_ref, table_ref, last):
    small = rim_ref.shape[0] // 2
    low, high = coarse_reach(w, small, near_ref.shape[0])
    reach = [(0, low, high), (1, low, high)] + ([(2, 0, 2 * small)] if last else [])
    rows = 0.0
    for s, low, high in reach:
        index = column_of(table_ref, COARSE + s, slice(w * span, (w + 1) * span))
        rows += mm(one_hot(index, high - low), (near_ref, far_ref, rim_ref)[s][low:high])
    return rows


def head_sums():
    block = 2 * LANES
    rows = lax.broadcasted_iota(jnp.int32, (block, block), 0) // (LANES // 2)
    cols = lax.broadcasted_iota(jnp.int32, (block, block), 1) // (LANES // 2)
    return (rows == cols).astype(jnp.float32).astype(jnp.bfloat16)


def mine_kernel(
    span,
    scale_ref,
    near_ref,
    far_ref,
    rim_ref,
    packed_ref,
    table_ref,
    own_ref,
    query_ref,
    key_ref,
    value_ref,
):
    windows = own_ref.shape[0] // span
    for w in range(windows):
        rows = coarse_rows(w, span, near_ref, far_ref, rim_ref, table_ref, w == windows - 1)
        own_ref[w * span : (w + 1) * span] = rows.astype(jnp.bfloat16)
    width = key_ref.shape[1]
    block = 2 * LANES
    same = head_sums()
    lane = lax.broadcasted_iota(jnp.int32, (1, block), 1)
    first = (lane % LANES < LANES // 2).astype(jnp.float32)
    head = lane // (LANES // 2)

    def multiply(task, _):
        start = "qkv".index(task[0]) * width + task[1] * block
        return mm(own_ref[...], packed_ref[:, start : start + block])

    def measure(task, rows):
        return rows, None if task[0] == "v" else mm((rows * rows).astype(jnp.bfloat16), same)

    def keep(task, held):
        kind, j = task
        rows, total = held
        at = slice(j * block, (j + 1) * block)
        if kind == "v":
            value_ref[:, at] = rows
            return
        rows = rows * lax.rsqrt(total + unit_eps)
        if kind == "k":
            key_ref[:, at] = rows
            return
        scale = jnp.zeros((1, block), jnp.float32)
        for h in range(2 * block // LANES):
            scale = jnp.where(head == h, scale_ref[j * 2 * block // LANES + h], scale)
        scale = scale * math.log2(math.e)
        left, right = rows * (scale * first), rows * (scale * (1.0 - first))
        for g in range(rows.shape[0] // GROUP):
            mine = slice(g * GROUP, (g + 1) * GROUP)
            query_ref[2 * g * GROUP : 2 * (g + 1) * GROUP, at] = jnp.concatenate(
                [left[mine], right[mine]], axis=0
            ).astype(jnp.bfloat16)

    staged([(k, j) for j in range(width // block) for k in "qkv"], [multiply, measure, keep])


def second_kernel(
    flags,
    own_ref,
    query_ref,
    own_key_ref,
    own_value_ref,
    other_near_ref,
    other_far_ref,
    other_rim_ref,
    packed_ref,
    output_ref,
    gain_ref,
    offset_ref,
    open_ref,
    table_ref,
    second_ref,
    send_ref,
    return_ref,
    return_near_ref,
    other,
    key,
    value,
    prob,
    ctx,
):
    span = open_ref.shape[0] * GROUP
    windows = own_ref.shape[0] // span
    for w in range(windows):
        rows = coarse_rows(
            w, span, other_near_ref, other_far_ref, other_rim_ref, table_ref, w == windows - 1
        )
        other[w * span : (w + 1) * span] = rows.astype(jnp.bfloat16)
    width = own_key_ref.shape[1]
    block = 2 * LANES
    same = head_sums()

    def multiply(task, _):
        start = "qkv".index(task[0]) * width + task[1] * block
        return mm(other[...], packed_ref[:, start : start + block])

    def measure(task, rows):
        return rows, None if task[0] == "v" else mm((rows * rows).astype(jnp.bfloat16), same)

    def keep(task, held):
        kind, j = task
        rows, total = held
        at = slice(j * block, (j + 1) * block)
        if kind == "k":
            rows = rows * lax.rsqrt(total + unit_eps)
        source, dst = (own_key_ref, key) if kind == "k" else (own_value_ref, value)
        for g in range(rows.shape[0] // GROUP):
            mine = slice(g * GROUP, (g + 1) * GROUP)
            dst[2 * g * GROUP : 2 * (g + 1) * GROUP, at] = jnp.concatenate(
                [source[mine, at], rows[mine]], axis=0
            ).astype(jnp.bfloat16)

    staged([(k, j) for j in range(width // block) for k in "kv"], [multiply, measure, keep])
    attend([None] * (windows - 1) + [flags[1]], query_ref, key, value, open_ref, prob, ctx)
    second = block_rows(own_ref, ctx, output_ref, gain_ref, offset_ref)
    second_ref[...] = second
    counts = [padded(ref.shape[0]) for ref in (send_ref, return_ref, return_near_ref)]
    index = parity_column(table_ref, SEND, 1, flags[2], slice(0, sum(counts)))
    rows = mm(one_hot(index, second.shape[0]), second).astype(jnp.bfloat16)
    at = 0
    for dst in (send_ref, return_ref, return_near_ref):
        count = dst.shape[0]
        dst[...] = rows[at : at + count]
        at += padded(count)


def place(pieces, out_ref, rows_ref, sem, low):
    rows, _, columns, pair, _ = rows_ref.shape
    block = sum(mm(one_hot(index, ref.shape[0]), ref[...]) for index, ref in pieces)
    copies = []
    for r in range(rows):
        for c in range(columns):
            at = (r * columns + c) * pair
            rows_ref[r, 0, c] = block[at : at + pair].astype(jnp.bfloat16)
        copies.append(pltpu.make_async_copy(rows_ref.at[r], out_ref.at[low + r], sem.at[r]))
        copies[-1].start()
    for copy in copies:
        copy.wait()


def place_columns(flags, table_ref, out_ref, which, early):
    step = out_ref.shape[2] * out_ref.shape[3]
    edge = HALF_LAT * step
    rows = slice(0, edge) if early else slice(edge, step * out_ref.shape[0])
    return [parity_column(table_ref, PLACE + s, 4, flags[2], rows) for s in which]


def late_kernel(flags, second_ref, near_ref, table_ref, out_ref, rows_ref, sem):
    index = place_columns(flags, table_ref, out_ref, (0, 1), False)
    place(zip(index, (second_ref, near_ref)), out_ref, rows_ref, sem, HALF_LAT)


def early_kernel(flags, back_ref, back_near_ref, table_ref, _, out_ref, rows_ref, sem):
    index = place_columns(flags, table_ref, out_ref, (2, 3), True)
    place(zip(index, (back_ref, back_near_ref)), out_ref, rows_ref, sem, 0)


def in_hbm(value):
    return pltpu.with_memory_space_constraint(value, pltpu.HBM)


def call(
    kernel, outs, scratch, scalars, operands, fixed=(), late=(), alias=None, held=False, room=SECOND_BYTES
):
    vmem = pl.BlockSpec(memory_space=pltpu.VMEM)
    hbm = pl.BlockSpec(memory_space=pltpu.HBM)
    fixed = [in_hbm(x) for x in fixed]
    return pl.pallas_call(
        kernel,
        out_shape=outs,
        in_specs=[pl.BlockSpec(memory_space=pltpu.SMEM)] * len(scalars)
        + [vmem] * len(operands)
        + [hbm] * len(fixed)
        + [vmem] * len(late),
        out_specs=[hbm if held else vmem] * len(outs),
        scratch_shapes=scratch,
        input_output_aliases=alias or {},
        compiler_params=pltpu.CompilerParams(vmem_limit_bytes=room),
    )(*scalars, *operands, *fixed, *late)


def far_of(i, n):
    return (i + (1 if i % 2 else -1)) % n


def near_swap(value):
    return lax.ppermute(value, "lon", [(i, i ^ 1) for i in range(lax.axis_size("lon"))])


def far_swap(value):
    n = lax.axis_size("lon")
    return lax.ppermute(value, "lon", [(i, far_of(i, n)) for i in range(n)])


def ring(value, by, turn):
    n, m = lax.axis_size("lat"), lax.axis_size("lon")
    links = [(i * m + j, (i + by) % n * m + turn(j, m)) for i in range(n) for j in range(m)]
    return lax.ppermute(value, ("lat", "lon"), links)


def shift(value, by):
    n = lax.axis_size("lat")
    return lax.ppermute(value, "lat", [(i, i + by) for i in range(n) if 0 <= i + by < n])


def body(
    features,
    packed_first,
    scale_first,
    output_first,
    gain_first,
    offset_first,
    merge_weight,
    merge_gain,
    merge_offset,
    packed_second,
    scale_second,
    output_second,
    gain_second,
    offset_second,
):
    levels, row_count, col_count, channels = features.shape
    inner = packed_first.shape[1] // 3
    second_inner = packed_second.shape[1] // 3
    wide = merge_weight.shape[1]
    half_rows = row_count // 2
    lat_pos = lax.axis_index("lat")
    odd = lax.axis_index("lon") % 2
    last = lax.axis_size("lat") - 1
    place = jnp.stack([lat_pos, lat_pos, 1 - odd])
    flags = (place == jnp.asarray([0, last, 1], jnp.int32)).astype(jnp.int32)
    bf16 = jnp.bfloat16
    span = levels // WLEV * GROUP
    tokens = HALF_LAT * levels * HALF_LON
    chunks = row_count // HALF_LAT
    windows = chunks // 2 + 1

    half = jax.ShapeDtypeStruct((chunks, tokens, channels), bf16)
    ends = jax.ShapeDtypeStruct((2, tokens, channels), bf16)
    near, far, ups, downs = call(
        split_kernel,
        [half, half, ends, ends],
        [pltpu.VMEM((levels, col_count, row_count, channels), bf16), pltpu.SemaphoreType.DMA],
        [flags],
        [],
        [jnp.transpose(features, (0, 2, 1, 3))],
    )
    bottom = shift(ups, -1)
    top = shift(downs, 1)
    near_other = near_swap(near)
    far_other = far_swap(far)
    near_other_top, near_other_bottom = near_swap(top), near_swap(bottom)
    far_rim = far_swap(jnp.stack([top[1], bottom[1]]))

    opened = jnp.asarray(open_tables(levels), bf16)
    cells = half_rows * levels * HALF_LON // 2
    small = jax.ShapeDtypeStruct((cells, wide), bf16)
    edge = jax.ShapeDtypeStruct((tokens, wide), bf16)

    shared = [packed_first, output_first, gain_first[None], offset_first[None]]
    shared += [merge_gain[None], merge_offset[None], opened]
    shared += [jnp.asarray(index_table(levels, row_count))]
    shared = call(
        load_kernel,
        [jax.ShapeDtypeStruct(x.shape, x.dtype) for x in shared],
        [pltpu.SemaphoreType.DMA((len(shared),))],
        [],
        [],
        shared,
    )
    shared = list(shared)
    opened, table = shared[-2:]
    buffers = [pltpu.VMEM(merge_weight.shape, bf16), pltpu.SemaphoreType.DMA]
    buffers += [pltpu.VMEM((windows * span, channels), bf16)]
    (inner_rows,) = call(
        inner_kernel,
        [jax.ShapeDtypeStruct(((windows - 2) * span, channels), bf16)],
        attention_scratch((windows - 2) * span, inner, channels),
        [in_hbm(scale_first)],
        [near, near_other] + shared[:4] + shared[-2:],
    )
    (merged_near,) = call(
        side_kernel,
        [small],
        buffers + attention_scratch(2 * span, inner, channels),
        [in_hbm(scale_first), flags],
        [near, near_other, top, bottom, near_other_top, near_other_bottom] + shared,
        [merge_weight],
        [inner_rows],
        room=FIRST_BYTES,
    )
    other_near = far_swap(merged_near)
    merged_far, edge_up = call(
        side_kernel,
        [small, edge],
        buffers + attention_scratch(windows * span, inner, channels),
        [in_hbm(scale_first), flags],
        [far, far_other, top, bottom, far_rim, far_rim] + shared,
        [merge_weight],
        [merged_near],
        room=FIRST_BYTES,
    )
    other_far = far_swap(merged_far)
    other_rim = ring(edge_up, -1, far_of)
    rim = ring(edge_up, -1, lambda j, m: j)

    windows = half_rows // WLAT
    share = levels // 2 * HALF_LON

    back = jax.ShapeDtypeStruct((HALF_LAT * share, wide), bf16)
    rows = windows * span
    mine = call(
        functools.partial(mine_kernel, span),
        [
            jax.ShapeDtypeStruct((rows, wide), bf16),
            jax.ShapeDtypeStruct((2 * rows, second_inner), bf16),
            jax.ShapeDtypeStruct((rows, second_inner), jnp.float32),
            jax.ShapeDtypeStruct((rows, second_inner), jnp.float32),
        ],
        [],
        [in_hbm(scale_second)],
        [merged_near, merged_far, rim, packed_second, table],
    )
    second, send, back_same, back_near = call(
        second_kernel,
        [
            jax.ShapeDtypeStruct((windows * span, wide), bf16),
            jax.ShapeDtypeStruct(((half_rows - HALF_LAT) * share, wide), bf16),
            back,
            back,
        ],
        [pltpu.VMEM((rows, wide), bf16)] + attention_scratch(rows, second_inner, wide)[3:],
        [flags],
        [
            *mine,
            other_near,
            other_far,
            other_rim,
            packed_second,
            output_second,
            gain_second[None],
            offset_second[None],
            opened,
            table,
        ],
    )
    back_near = ring(back_near, 1, lambda j, m: j ^ 1)
    back_same = ring(back_same, 1, lambda j, m: j)
    received = near_swap(send)
    shape = (half_rows, 1, WLON, levels // 2, wide)
    whole = [jax.ShapeDtypeStruct(shape, bf16)]

    def room(rows):
        return [pltpu.VMEM((rows,) + shape[1:], bf16), pltpu.SemaphoreType.DMA((rows,))]

    (out,) = call(
        late_kernel,
        whole,
        room(half_rows - HALF_LAT),
        [flags],
        [second, received, table],
        held=True,
    )
    (out,) = call(
        early_kernel,
        whole,
        room(HALF_LAT),
        [flags],
        [back_same, back_near, table],
        [out],
        alias={4: 0},
        held=True,
    )
    return jnp.transpose(out, (0, 1, 3, 2, 4))


def solution(mesh):
    return jax.shard_map(
        body,
        mesh=mesh,
        in_specs=(P(None, "lat", "lon", None),) + (P(),) * 13,
        out_specs=P("lat", "lon", None, None, None),
        check_vma=False,
    )
```
